32 devices in a mesh: strip: 8 (over y, x, core), view: 4 (over z).
Axes of the slice: x: 2, y: 2, z: 4, core: 2. Of those that a mesh axis runs over, the one named last changes fastest.
Arguments:
- images: bfloat16 [4, 1024, 640], P('view', 'strip'), may hold values from -6 to 6
- offsets: int32 [4, 8], P(None, 'strip'), may hold values from 0 to 376
- pair_step: int32 [8], P('strip'), may hold values from 1 to 3
- row_map: int32 [1024], replicated, may hold values from 0 to 1023, as said below
Outputs:
- cost_volume: bfloat16 [4, 128, 1024, 128], P('view', None, 'strip')
The draws below stay inside these ranges and needn't reach their ends.
Inputs may be any that keep to these rules, and one draw needn't show every extreme that they name: `row_map`: A permutation of the 1024 rows. Of the 128 entries in each aligned block of 128 tile rows, exactly 16 fall in each aligned block of 128 strip rows.
All inputs are finite; a program needn't handle non-finite values.
Results may differ from the reference program's by a relative error of at most 0.001.
Values may be sent and summed in bfloat16 or wider, within the bound.
No kernel may reach another device: no remote copies, remote signals or barrier semaphores. Data moves between devices by JAX's collectives and lax.ppermute only.
A program may use at most 64 MiB of HBM per device.

```python
import jax
import jax.numpy as jnp
from jax import lax

COLS = 128
ROWS_DEV = 128
DISP = 128
OFF_MAX = 376
VIEWS = 4
STRIPS = 8
ROWS = 1024
WIDE = 640
SPAN = 264


def draw_row_map(key, part):
    strip_count = ROWS // ROWS_DEV
    per_peer = ROWS_DEV // strip_count
    first_key, second_key = jax.random.split(jax.random.fold_in(key, 11))
    source_order = jax.vmap(lambda one_key: jax.random.permutation(one_key, ROWS_DEV))(jax.random.split(first_key, strip_count)).astype(jnp.int32)
    target_slots = jax.vmap(lambda one_key: jax.random.permutation(one_key, ROWS_DEV))(jax.random.split(second_key, strip_count)).astype(jnp.int32)
    source_ids = jnp.arange(strip_count, dtype=jnp.int32)[:, None]
    target_ids = source_order // per_peer
    within = source_order % per_peer
    slot_ids = target_slots[target_ids, source_ids * per_peer + within]
    return (target_ids * ROWS_DEV + slot_ids).reshape(ROWS).astype(jnp.int32)


def plant(values, stream_key, least, high):
    longest = values.shape.index(max(values.shape))
    spots = []
    for shift in (0, 1):
        where = [jax.random.randint(jax.random.fold_in(stream_key, axis), (), 0, length) for axis, length in enumerate(values.shape)]
        where[longest] = (where[longest] + shift) % values.shape[longest]
        spots.append(tuple(where))
    return values.at[spots[0]].set(least).at[spots[1]].set(high)


def level_of(key, shape, cuts, low, largest):
    loudness, own = 1.0, jax.random.fold_in(key, 6)
    for axis_at, blocks in cuts:
        steps = jnp.exp(jax.random.uniform(jax.random.fold_in(own, axis_at), (blocks,), jnp.float32, low / len(cuts), largest / len(cuts)))
        loudness = loudness * jnp.repeat(steps, shape[axis_at] // blocks).reshape([-1 if axis == axis_at else 1 for axis in range(len(shape))])
    return loudness


def gaussian(own_key, shape, deviation, limit, shards=(), kind=jnp.bfloat16):
    values = deviation * jax.random.normal(own_key, shape, jnp.float32)
    if shards:
        values = values * level_of(own_key, shape, shards, -0.22, 0.18)
    return jnp.clip(values, -limit, limit).astype(kind)


def setup_inputs(seed: int = 0) -> dict:
    seeds = jax.random.split(jax.random.key(seed), 5)
    return {
        "images": gaussian(seeds[0], (VIEWS, ROWS, WIDE), 1.0, 6.0, ((0, 4), (1, 8))),
        "offsets": plant(jax.random.randint(seeds[1], (VIEWS, STRIPS), 0, OFF_MAX + 1), jax.random.fold_in(seeds[1], 1), 0, OFF_MAX).astype(jnp.int32),
        "pair_step": plant(jax.random.randint(seeds[2], (STRIPS,), 1, VIEWS), jax.random.fold_in(seeds[2], 1), 1, VIEWS - 1).astype(jnp.int32),
        "row_map": draw_row_map(jax.random.fold_in(seeds[4], 71), 0),
    }


EPSILON = 1e-05

def box_sum(values):
    out_rows = values.shape[-2] - 8
    out_cols = values.shape[-1] - 8
    row_sums = values[..., 0:out_rows, :]
    for shift_row in range(1, 9):
        row_sums = row_sums + values[..., shift_row:shift_row + out_rows, :]
    box_total = row_sums[..., 0:out_cols]
    for shift_col in range(1, 9):
        box_total = box_total + row_sums[..., shift_col:shift_col + out_cols]
    return box_total

def cost_block(ref_window, mate_window):
    ref_float = ref_window.astype(jnp.float32)
    mate_float = mate_window.astype(jnp.float32)
    rows_out = ref_window.shape[0] - 8
    cols_out = ref_window.shape[1] - 8
    sum_ref = box_sum(ref_float)
    sum_ref_sq = box_sum(ref_float * ref_float)
    mean_ref = sum_ref / 81.0
    var_ref = sum_ref_sq / 81.0 - mean_ref * mean_ref
    mate_box = box_sum(mate_float)
    mate_box_sq = box_sum(mate_float * mate_float)

    def block_step(block_index, volume):
        first_disp = (block_index * 16).astype(jnp.int32)
        starts = [DISP - 1 - within - first_disp for within in range(16)]
        shifted = jnp.stack([lax.dynamic_slice_in_dim(mate_float, begin, cols_out + 8, 1) for begin in starts])
        sum_cross = box_sum(ref_float[None] * shifted)
        sum_mate = jnp.stack([lax.dynamic_slice_in_dim(mate_box, begin, cols_out, 1) for begin in starts])
        sum_mate_sq = jnp.stack([lax.dynamic_slice_in_dim(mate_box_sq, begin, cols_out, 1) for begin in starts])
        mean_mate = sum_mate / 81.0
        var_mate = sum_mate_sq / 81.0 - mean_mate * mean_mate
        covariance = sum_cross / 81.0 - mean_ref * mean_mate
        ncc_score = covariance * lax.rsqrt((var_ref + EPSILON) * (var_mate + EPSILON))
        return lax.dynamic_update_slice_in_dim(volume, ncc_score.astype(jnp.bfloat16), first_disp, 0)
    empty = jnp.zeros((DISP, rows_out, cols_out), jnp.bfloat16)
    return lax.fori_loop(0, DISP // 16, block_step, empty)

def reference(images, offsets, pair_step, row_map):
    strip_count = ROWS // ROWS_DEV
    regrouped = jnp.zeros_like(images).at[:, row_map, :].set(images)
    padded = jnp.pad(regrouped, ((0, 0), (4, 4), (0, 0)))
    result = jnp.zeros((VIEWS, DISP, ROWS, COLS), jnp.bfloat16)

    def one_item(item, volume_all):
        item = jnp.asarray(item).astype(jnp.int32)
        view_id = item // strip_count
        strip_id = item % strip_count
        mate_id = ((view_id + pair_step[strip_id]) % VIEWS).astype(jnp.int32)
        offset_now = offsets[view_id, strip_id].astype(jnp.int32)
        row_start = (strip_id * ROWS_DEV).astype(jnp.int32)
        zero_index = jnp.zeros((), jnp.int32)
        own_rows = lax.dynamic_slice(padded, (view_id, row_start, zero_index), (1, ROWS_DEV + 8, WIDE))[0]
        mate_start = (OFF_MAX - offset_now).astype(jnp.int32)
        mate_rows = lax.dynamic_slice(padded, (mate_id, row_start, mate_start), (1, ROWS_DEV + 8, SPAN))[0]
        ref_window = own_rows[:, OFF_MAX + DISP - 1:OFF_MAX + DISP - 1 + COLS + 8]
        volume = cost_block(ref_window, mate_rows)
        return lax.dynamic_update_slice(volume_all, volume[None], (view_id, zero_index, row_start, zero_index))
    return lax.fori_loop(0, VIEWS * strip_count, one_item, result)
```

```python
import functools

import jax
import jax.numpy as jnp
from jax import lax
from jax.experimental import pallas as pl
from jax.experimental.pallas import tpu as pltpu
from jax.sharding import PartitionSpec as P

COLS = 128
DISP = 128
OFF_MAX = 376


EPSILON = 1e-05


def for_sending(value):

    def short(part):
        return part.astype(jnp.bfloat16) if part.dtype == jnp.float32 else part

    return jax.tree.map(short, value)


def passed_along(value, axis, by):
    size = lax.axis_size(axis)
    return lax.ppermute(value, axis, [(i, (i + by) % size) for i in range(size)])


def with_halo(cells, sides, width):
    for axis, dim in sides:
        count = lax.axis_size(axis)
        ends = count - 1
        head = lax.slice_in_dim(cells, 0, width, axis=dim)
        tail = lax.slice_in_dim(cells, cells.shape[dim] - width, cells.shape[dim], axis=dim)
        cells = jnp.concatenate(
            [
                lax.ppermute(tail, axis, [(i, (i + 1) % count) for i in range(ends)]),
                cells,
                lax.ppermute(head, axis, [((i + 1) % count, i) for i in range(ends)]),
            ],
            axis=dim,
        )
    return cells


RB=16
UN=8
PITCH=17

def cost_kernel(ref_ref, mate_ref, out_ref, ref32, mate32, H, S, hm, hq, rm, ra, *, rows):
    g = pl.program_id(0)
    f32=jnp.float32; bf=jnp.bfloat16
    i0 = lax.broadcasted_iota(jnp.int32,(128,128),0)
    i1 = lax.broadcasted_iota(jnp.int32,(128,128),1)
    d1 = i1 - i0
    band1 = ((d1>=0)&(d1<=8)).astype(bf)
    d2 = 16 + i1 - i0
    band2 = ((d2>=0)&(d2<=8)&(i1>=112)).astype(bf)

    @pl.when(g==0)
    def _():
        ref32[...] = ref_ref[...].astype(f32)
        mate32[...] = mate_ref[...].astype(f32)
        kk = lax.broadcasted_iota(jnp.int32,(384,256),0)
        cc = lax.broadcasted_iota(jnp.int32,(384,256),1)
        box = ((kk-cc>=0)&(kk-cc<=8)).astype(bf)
        def boxes(x, w):
            p = x.astype(f32)*x.astype(f32)
            hi = p.astype(bf)
            lo = (p - hi.astype(f32)).astype(bf)
            s = jnp.dot(x, w, preferred_element_type=f32)
            q = jnp.dot(hi, w, preferred_element_type=f32)+jnp.dot(lo, w, preferred_element_type=f32)
            return s,q
        s,q = boxes(mate_ref[...], box)
        hm[0] = s[:, :128]; hm[1]=s[:,128:]; hq[0] = q[:, :128]; hq[1]=q[:,128:]
        kr = lax.broadcasted_iota(jnp.int32,(256,128),0)
        cr = lax.broadcasted_iota(jnp.int32,(256,128),1)
        dr = jnp.where(kr<128, kr, kr-112) - cr
        boxr = ((dr>=0)&(dr<=8)&((kr<128)|(kr>=240))).astype(bf)
        s,q = boxes(ref_ref[...], boxr)
        rm[...] = s; ra[...] = q

    def one_row(r):
        m = jnp.broadcast_to(mate32[pl.ds(r,1),:], (16,384))
        base = pltpu.roll(m, 1, axis=1, stride=1, stride_axis=0).astype(bf)
        t = [base[:, 128*i:128*i+128] for i in range(3)]
        lane = lax.broadcasted_iota(jnp.int32,(16,128),1)
        tiles=[]
        for p in range(-1,8):
            o = 128-16*p
            a, b = divmod(o,128)
            if b==0:
                w = t[a]
            else:
                w = jnp.where(lane>=b, t[a], t[a+1])
                w = pltpu.roll(w.astype(f32), 128-b, axis=1).astype(bf)
            tiles.append(w)
        left = jnp.concatenate(tiles[1:],axis=0)
        right = jnp.concatenate(tiles[:-1],axis=0)
        rr = ref32[pl.ds(r,1),:].astype(bf)
        w1 = band1*jnp.broadcast_to(rr[:, :128],(128,128))
        rsh = rr[:, 128:]
        w2 = band2*jnp.broadcast_to(rsh,(128,128))
        lhs = jnp.concatenate([left,right],axis=1)
        rhs = jnp.concatenate([w1,w2],axis=1)
        return lax.dot_general(lhs, rhs, (((1,),(1,)),((),())), preferred_element_type=f32)

    lo = jnp.where(g==0, 0, (RB*g+8)//UN)
    hi = (RB*g+RB+8)//UN
    def body(it, c):
        for j in range(UN):
            r = it*UN+j
            H[r] = one_row(r)
        return c
    lax.fori_loop(lo, hi, body, 0)

    r0 = RB*g
    def vq(q, c):
        h = [H[r0+i, pl.ds(pl.multiple_of(8*q,8),8), :] for i in range(RB+8)]
        out=[None]*RB
        for b0 in range(0, RB, 9):
            n = min(9, RB-b0)
            suf=[None]*9
            suf[8]=h[b0+8]
            for i in range(7,-1,-1): suf[i]=h[b0+i]+suf[i+1]
            out[b0]=suf[0]
            pre=None
            for i in range(1,n):
                pre = h[b0+8+i] if pre is None else pre+h[b0+8+i]
                out[b0+i]=suf[i]+pre
        for i in range(RB):
            S[pl.ds(8*q*PITCH+i, 8, stride=PITCH), :] = out[i]
        return c
    lax.fori_loop(0, 16, vq, 0)

    def vert(ref):
        x = [ref[pl.ds(r0+i, RB), :] for i in range(9)]
        return ((x[0]+x[1])+(x[2]+x[3]))+((x[4]+x[5])+(x[6]+x[7]))+x[8]
    sr = vert(rm); srr = vert(ra)
    mr = sr/81.0
    ar = lax.rsqrt(jnp.maximum(srr/81.0-mr*mr,0.0)+EPSILON)
    sm0 = vert(hm.at[0]); sm1=vert(hm.at[1])
    def inv(s, q):
        mm = s/81.0
        return lax.rsqrt(jnp.maximum(q/81.0-mm*mm,0.0)+EPSILON)/81.0
    am0 = inv(sm0, vert(hq.at[0])); am1 = inv(sm1, vert(hq.at[1]))
    lane = lax.broadcasted_iota(jnp.int32,(RB,128),1)
    for k in range(128):
        o = 127-k
        x, y = sm0, am0
        if o:
            keep = lane>=o
            x = pltpu.roll(jnp.where(keep, sm0, sm1), 128-o, axis=1)
            y = pltpu.roll(jnp.where(keep, am0, am1), 128-o, axis=1)
        s = S[pl.ds(k*PITCH, RB), :]
        v = (s - mr*x)*ar*y
        out_ref[k] = v.astype(bf)

def cost(ref_in, mate_in):
    rows = ref_in.shape[0]-8
    f32=jnp.float32
    return pl.pallas_call(
        functools.partial(cost_kernel, rows=rows),
        out_shape=jax.ShapeDtypeStruct((DISP, rows, COLS), jnp.bfloat16),
        grid=(rows//RB,),
        in_specs=[pl.BlockSpec((rows+8,256), lambda g:(0,0)), pl.BlockSpec((rows+8,384), lambda g:(0,0))],
        out_specs=pl.BlockSpec((DISP, RB, COLS), lambda g:(0,g,0)),
        scratch_shapes=[pltpu.VMEM((rows+8,256),f32), pltpu.VMEM((rows+8,384),f32),
            pltpu.VMEM((rows+8,128,128),f32), pltpu.VMEM((128*PITCH,128),f32),
            pltpu.VMEM((2,rows+8,128),f32), pltpu.VMEM((2,rows+8,128),f32),
            pltpu.VMEM((rows+8,128),f32), pltpu.VMEM((rows+8,128),f32)],
        compiler_params=pltpu.CompilerParams(dimension_semantics=("arbitrary",), vmem_limit_bytes=48<<20),
        name="cost_volume",
    )(ref_in, mate_in)

def prep(ref_window, mate_window):
    r = jnp.concatenate([ref_window[:, :128], jnp.pad(ref_window[:, 16:136],((0,0),(0,8)))], axis=1)
    return r, jnp.pad(mate_window, ((0,0),(0,120)))


def rotate_by(step_size, view_me, view_count, offsets, span_cols):

    def branch(own_rows):
        receiver = (view_me - step_size) % view_count
        slab = lax.dynamic_slice_in_dim(own_rows, OFF_MAX - offsets[receiver, 0], span_cols, 1)
        return passed_along(for_sending(slab), "view", view_count - step_size).astype(slab.dtype)

    return branch


def shards(images, offsets, pair_step, row_map):
    own_tiles = images[0]
    rows_dev = own_tiles.shape[0]
    width_all = own_tiles.shape[1]
    span_cols = COLS + DISP + 8
    strip_count = lax.axis_size("strip")
    view_count = lax.axis_size("view")
    strip_me = lax.axis_index("strip")
    view_me = lax.axis_index("view")
    per_peer = rows_dev // strip_count
    local_map = lax.dynamic_slice_in_dim(row_map, strip_me * rows_dev, rows_dev)
    targets = local_map // rows_dev
    send_order = jnp.argsort(targets, stable=True)
    outgoing = own_tiles[send_order].reshape(strip_count, per_peer, width_all)
    arrived = lax.all_to_all(outgoing, "strip", split_axis=0, concat_axis=0, tiled=True)
    whole_table = row_map.reshape(strip_count, rows_dev)
    hits = whole_table // rows_dev == strip_me
    column_ids = lax.broadcasted_iota(jnp.int32, whole_table.shape, 1)
    rank_keys = jnp.where(hits, column_ids, column_ids + rows_dev)
    picked = jnp.argsort(rank_keys, axis=1, stable=True)[:, :per_peer]
    slot_ids = jnp.take_along_axis(whole_table % rows_dev, picked, axis=1).reshape(rows_dev)
    inverse = jnp.argsort(slot_ids)
    strip_rows = arrived.reshape(rows_dev, width_all)[inverse]
    bordered = with_halo(strip_rows[None], (("strip", 1),), 4)
    own_rows = bordered[0]
    step_now = pair_step[0] % view_count
    branches = [
        rotate_by(step_size, view_me, view_count, offsets, span_cols)
        for step_size in range(1, view_count)
    ]
    mate_window = lax.switch(step_now - 1, branches, own_rows)
    ref_window = own_rows[:, OFF_MAX + DISP - 1 : OFF_MAX + DISP - 1 + COLS + 8]
    volume = cost(*prep(ref_window, mate_window))
    return volume[None]


def solution(mesh):
    in_specs = (P("view", "strip", None), P(None, "strip"), P("strip"), P())
    out_specs = P("view", None, "strip", None)
    return jax.shard_map(shards, mesh=mesh, in_specs=in_specs, out_specs=out_specs, check_vma=False)
```

```python
import functools

import jax
import jax.numpy as jnp
from jax import lax
from jax.experimental import pallas as pl
from jax.experimental.pallas import tpu as pltpu
from jax.sharding import PartitionSpec as P

COLS = 128
DISP = 128
OFF_MAX = 376


EPSILON = 1e-05


RB=16
UN=8
PITCH=17

def cost_kernel(ref_ref, mate_ref, out_ref, ref32, mate32, H, S, hm, hq, rm, ra, *, rows):
    g = pl.program_id(0)
    f32=jnp.float32; bf=jnp.bfloat16
    i0 = lax.broadcasted_iota(jnp.int32,(128,128),0)
    i1 = lax.broadcasted_iota(jnp.int32,(128,128),1)
    d1 = i1 - i0
    band1 = ((d1>=0)&(d1<=8)).astype(bf)
    d2 = 16 + i1 - i0
    band2 = ((d2>=0)&(d2<=8)&(i1>=112)).astype(bf)

    @pl.when(g==0)
    def _():
        ref32[...] = ref_ref[...].astype(f32)
        mate32[...] = mate_ref[...].astype(f32)
        kk = lax.broadcasted_iota(jnp.int32,(384,256),0)
        cc = lax.broadcasted_iota(jnp.int32,(384,256),1)
        box = ((kk-cc>=0)&(kk-cc<=8)).astype(bf)
        def boxes(x, w):
            p = x.astype(f32)*x.astype(f32)
            hi = p.astype(bf)
            lo = (p - hi.astype(f32)).astype(bf)
            s = jnp.dot(x, w, preferred_element_type=f32)
            q = jnp.dot(hi, w, preferred_element_type=f32)+jnp.dot(lo, w, preferred_element_type=f32)
            return s,q
        s,q = boxes(mate_ref[...], box)
        hm[0] = s[:, :128]; hm[1]=s[:,128:]; hq[0] = q[:, :128]; hq[1]=q[:,128:]
        kr = lax.broadcasted_iota(jnp.int32,(256,128),0)
        cr = lax.broadcasted_iota(jnp.int32,(256,128),1)
        dr = jnp.where(kr<128, kr, kr-112) - cr
        boxr = ((dr>=0)&(dr<=8)&((kr<128)|(kr>=240))).astype(bf)
        s,q = boxes(ref_ref[...], boxr)
        rm[...] = s; ra[...] = q

    def one_row(r):
        m = jnp.broadcast_to(mate32[pl.ds(r,1),:], (16,384))
        base = pltpu.roll(m, 1, axis=1, stride=1, stride_axis=0).astype(bf)
        t = [base[:, 128*i:128*i+128] for i in range(3)]
        lane = lax.broadcasted_iota(jnp.int32,(16,128),1)
        tiles=[]
        for p in range(-1,8):
            o = 128-16*p
            a, b = divmod(o,128)
            if b==0:
                w = t[a]
            else:
                w = jnp.where(lane>=b, t[a], t[a+1])
                w = pltpu.roll(w.astype(f32), 128-b, axis=1).astype(bf)
            tiles.append(w)
        left = jnp.concatenate(tiles[1:],axis=0)
        right = jnp.concatenate(tiles[:-1],axis=0)
        rr = ref32[pl.ds(r,1),:].astype(bf)
        w1 = band1*jnp.broadcast_to(rr[:, :128],(128,128))
        rsh = rr[:, 128:]
        w2 = band2*jnp.broadcast_to(rsh,(128,128))
        lhs = jnp.concatenate([left,right],axis=1)
        rhs = jnp.concatenate([w1,w2],axis=1)
        return lax.dot_general(lhs, rhs, (((1,),(1,)),((),())), preferred_element_type=f32)

    lo = jnp.where(g==0, 0, (RB*g+8)//UN)
    hi = (RB*g+RB+8)//UN
    def body(it, c):
        for j in range(UN):
            r = it*UN+j
            H[r] = one_row(r)
        return c
    lax.fori_loop(lo, hi, body, 0)

    r0 = RB*g
    def vq(q, c):
        h = [H[r0+i, pl.ds(pl.multiple_of(8*q,8),8), :] for i in range(RB+8)]
        out=[None]*RB
        for b0 in range(0, RB, 9):
            n = min(9, RB-b0)
            suf=[None]*9
            suf[8]=h[b0+8]
            for i in range(7,-1,-1): suf[i]=h[b0+i]+suf[i+1]
            out[b0]=suf[0]
            pre=None
            for i in range(1,n):
                pre = h[b0+8+i] if pre is None else pre+h[b0+8+i]
                out[b0+i]=suf[i]+pre
        for i in range(RB):
            S[pl.ds(8*q*PITCH+i, 8, stride=PITCH), :] = out[i]
        return c
    lax.fori_loop(0, 16, vq, 0)

    def vert(ref):
        x = [ref[pl.ds(r0+i, RB), :] for i in range(9)]
        return ((x[0]+x[1])+(x[2]+x[3]))+((x[4]+x[5])+(x[6]+x[7]))+x[8]
    sr = vert(rm); srr = vert(ra)
    mr = sr/81.0
    ar = lax.rsqrt(jnp.maximum(srr/81.0-mr*mr,0.0)+EPSILON)
    sm0 = vert(hm.at[0]); sm1=vert(hm.at[1])
    def inv(s, q):
        mm = s/81.0
        return lax.rsqrt(jnp.maximum(q/81.0-mm*mm,0.0)+EPSILON)/81.0
    am0 = inv(sm0, vert(hq.at[0])); am1 = inv(sm1, vert(hq.at[1]))
    lane = lax.broadcasted_iota(jnp.int32,(RB,128),1)
    for k in range(128):
        o = 127-k
        x, y = sm0, am0
        if o:
            keep = lane>=o
            x = pltpu.roll(jnp.where(keep, sm0, sm1), 128-o, axis=1)
            y = pltpu.roll(jnp.where(keep, am0, am1), 128-o, axis=1)
        s = S[pl.ds(k*PITCH, RB), :]
        v = (s - mr*x)*ar*y
        out_ref[k] = v.astype(bf)

def cost(ref_in, mate_in):
    rows = ref_in.shape[0]-8
    f32=jnp.float32
    return pl.pallas_call(
        functools.partial(cost_kernel, rows=rows),
        out_shape=jax.ShapeDtypeStruct((DISP, rows, COLS), jnp.bfloat16),
        grid=(rows//RB,),
        in_specs=[pl.BlockSpec((rows+8,256), lambda g:(0,0)), pl.BlockSpec((rows+8,384), lambda g:(0,0))],
        out_specs=pl.BlockSpec((DISP, RB, COLS), lambda g:(0,g,0)),
        scratch_shapes=[pltpu.VMEM((rows+8,256),f32), pltpu.VMEM((rows+8,384),f32),
            pltpu.VMEM((rows+8,128,128),f32), pltpu.VMEM((128*PITCH,128),f32),
            pltpu.VMEM((2,rows+8,128),f32), pltpu.VMEM((2,rows+8,128),f32),
            pltpu.VMEM((rows+8,128),f32), pltpu.VMEM((rows+8,128),f32)],
        compiler_params=pltpu.CompilerParams(dimension_semantics=("arbitrary",), vmem_limit_bytes=48<<20),
        name="cost_volume",
    )(ref_in, mate_in)

SPAN = COLS + DISP + 8
EDGE = 4
REF_FROM = OFF_MAX + DISP - 1


def slot_count(rows_dev, strips):
    wide = rows_dev // strips + 2 * EDGE
    return -(-wide // 8) * 8


def places(ids, low, rows_dev):
    line = ids.shape[1]
    place = ids - low + EDGE
    wanted = (place >= 0) & (place < rows_dev + 2 * EDGE)
    before = lax.broadcasted_iota(jnp.int32, (line, line), 0)
    after = lax.broadcasted_iota(jnp.int32, (line, line), 1)
    earlier = (before < after).astype(jnp.bfloat16)
    flags = jnp.where(wanted, 1.0, 0.0)
    pad = (-flags.shape[0]) % 16
    if pad:
        flags = jnp.concatenate([flags, jnp.zeros((pad, line), jnp.float32)], axis=0)
    rank = jnp.dot(flags.astype(jnp.bfloat16), earlier, preferred_element_type=jnp.float32)
    rank = rank[: ids.shape[0]].astype(jnp.int32)
    return jnp.where(wanted, rank, -1), place


def spread(rank, slots):
    strips, line = rank.shape
    wide = jnp.broadcast_to(rank[:, None, :], (strips, slots, line))
    return wide == lax.broadcasted_iota(jnp.int32, (strips, slots, line), 1)


def pack_kernel(map_ref, tiles_ref, out_ref):
    strips, slots, width = out_ref.shape
    rows_dev = tiles_ref.shape[0]
    ids = jnp.broadcast_to(map_ref[...], (strips, rows_dev))
    low = rows_dev * lax.broadcasted_iota(jnp.int32, (strips, rows_dev), 0)
    rank, _ = places(ids, low, rows_dev)
    pick = jnp.where(spread(rank, slots), 1.0, 0.0).reshape(strips * slots, rows_dev).astype(jnp.bfloat16)
    rows = jnp.dot(pick, tiles_ref[...], preferred_element_type=jnp.float32)
    out_ref[...] = rows.astype(jnp.bfloat16).reshape(out_ref.shape)


def table_kernel(table_ref, out_ref):
    strips, rows_dev = table_ref.shape
    rows, positions = out_ref.shape
    slots = positions // strips
    low = rows_dev * lax.axis_index("strip")
    rank, place = places(table_ref[...], low, rows_dev)
    wide = jnp.broadcast_to(place[:, None, :], (strips, slots, rows_dev))
    named = jnp.where(spread(rank, slots), wide + 1, 0).astype(jnp.float32)
    named = named.reshape(positions, rows_dev).astype(jnp.bfloat16)
    ones = jnp.ones((16, rows_dev), jnp.bfloat16)
    target = lax.dot_general(ones, named, (((1,), (1,)), ((), ())), preferred_element_type=jnp.float32)
    target = jnp.broadcast_to(target[:1].astype(jnp.int32), (rows, positions))
    mine = lax.broadcasted_iota(jnp.int32, (rows, positions), 0) + 1
    out_ref[...] = jnp.where(target == mine, 1.0, 0.0).astype(jnp.bfloat16)


def unpack_kernel(offsets_ref, step_ref, table_ref, arrived_ref, ref_ref, slab_ref, strip):
    rows = ref_ref.shape[0]
    width = arrived_ref.shape[1]
    views = offsets_ref.shape[0]
    own = jnp.dot(table_ref[...], arrived_ref[...], preferred_element_type=jnp.float32)
    strip[:, :width] = own
    strip[:, width:] = jnp.zeros((rows, strip.shape[1] - width), jnp.float32)
    ref_ref[:, :128] = own[:, REF_FROM : REF_FROM + 128].astype(jnp.bfloat16)
    ref_ref[:, 128:] = strip[:, REF_FROM + 16 : REF_FROM + 144].astype(jnp.bfloat16)
    receiver = lax.rem(lax.axis_index("view") + views - lax.rem(step_ref[0], views), views)
    start = jnp.clip(OFF_MAX - offsets_ref[receiver, 0], 0, OFF_MAX)
    whole = start // 128
    part = start - whole * 128
    block = strip[:, pl.ds(pl.multiple_of(whole * 128, 128), 512)]
    turned = pltpu.roll(block, 512 - part, axis=1)
    slab_ref[...] = turned[:, :384].astype(jnp.bfloat16)


def shards(images, offsets, pair_step, row_map):
    own_tiles = images[0]
    rows_dev, width = own_tiles.shape
    strips = lax.axis_size("strip")
    views = lax.axis_size("view")
    strip_me = lax.axis_index("strip")
    slots = slot_count(rows_dev, strips)
    rows = rows_dev + 2 * EDGE
    bf16 = jnp.bfloat16
    table = row_map.reshape(strips, rows_dev)
    local = lax.dynamic_slice_in_dim(table, strip_me, 1)
    outgoing = pl.pallas_call(
        pack_kernel, out_shape=jax.ShapeDtypeStruct((strips, slots, width), bf16), name="pack"
    )(local, own_tiles)
    arrived = lax.all_to_all(outgoing, "strip", split_axis=0, concat_axis=0, tiled=True)
    select = pl.pallas_call(
        table_kernel, out_shape=jax.ShapeDtypeStruct((rows, strips * slots), bf16), name="table"
    )(table)
    smem = pl.BlockSpec(memory_space=pltpu.SMEM)
    vmem = pl.BlockSpec(memory_space=pltpu.VMEM)
    ref_rows, slab = pl.pallas_call(
        unpack_kernel,
        out_shape=(jax.ShapeDtypeStruct((rows, 256), bf16), jax.ShapeDtypeStruct((rows, 384), bf16)),
        in_specs=[smem, smem, vmem, vmem],
        scratch_shapes=[pltpu.VMEM((rows, 768), jnp.float32)],
        name="unpack",
    )(offsets, pair_step, select, arrived.reshape(strips * slots, width))

    def sent_by(step):
        return lambda rows_out: lax.ppermute(rows_out, "view", [(i, (i - step) % views) for i in range(views)])

    mate_rows = lax.switch(pair_step[0] % views - 1, [sent_by(step) for step in range(1, views)], slab)
    return cost(ref_rows, mate_rows)[None]


def solution(mesh):
    in_specs = (P("view", "strip", None), P(None, "strip"), P("strip"), P())
    out_specs = P("view", None, "strip", None)
    return jax.shard_map(shards, mesh=mesh, in_specs=in_specs, out_specs=out_specs, check_vma=False)
```

```python
import functools

import jax
import jax.numpy as jnp
from jax import lax
from jax.experimental import pallas as pl
from jax.experimental.pallas import tpu as pltpu
from jax.sharding import PartitionSpec as P

COLS = 128
DISP = 128
OFF_MAX = 376


EPSILON = 1e-05


RB = 16
PITCH = 17
PIECES = 2


def box_sums(values, weights):
    f32, bf16 = jnp.float32, jnp.bfloat16
    wide = values.astype(f32)
    square = wide * wide
    high = square.astype(bf16)
    low = (square - high.astype(f32)).astype(bf16)
    total = jnp.dot(values, weights, preferred_element_type=f32)
    total_sq = jnp.dot(high, weights, preferred_element_type=f32)
    return total, total_sq + jnp.dot(low, weights, preferred_element_type=f32)


def cost_kernel(ref_ref, mate_ref, out_ref, ref32, mate32, base, lines_a, lines_b, last_a, last_b, sums, sent, sems,
                mate_sum, mate_sq, ref_sum, ref_sq):
    step = pl.program_id(0)
    rows = ref_ref.shape[0]
    f32, bf16 = jnp.float32, jnp.bfloat16
    down = lax.broadcasted_iota(jnp.int32, (128, 128), 0)
    across = lax.broadcasted_iota(jnp.int32, (128, 128), 1)
    gap = across - down
    band_near = ((gap >= 0) & (gap <= 8)).astype(bf16)
    band_far = ((gap >= -16) & (gap <= -8) & (across >= 112)).astype(bf16)
    lane = lax.broadcasted_iota(jnp.int32, (RB, 128), 1)

    def skew(first, count):
        block = mate32[pl.ds(first, count), :]
        for s in range(16):
            turned = pltpu.roll(block, 1 + s, axis=1)
            for t in range(3):
                for r in range(0, count, 8):
                    base[t, pl.ds(r * PITCH + s, 8, stride=PITCH), :] = turned[r : r + 8, 128 * t : 128 * t + 128]

    def one_line(first, r):
        tiles = [base[t, pl.ds(r * PITCH, 16), :].astype(bf16) for t in range(3)]
        parts = []
        for p in range(-1, 8):
            a, b = divmod(128 - 16 * p, 128)
            if b == 0:
                part = tiles[a]
            else:
                part = pltpu.roll(jnp.where(lane >= b, tiles[a], tiles[a + 1]), 128 - b, axis=1)
            parts.append(part)
        near = jnp.concatenate(parts[1:], axis=0)
        far = jnp.concatenate(parts[:-1], axis=0)
        row = ref32[pl.ds(first + r, 1), :].astype(bf16)
        left = jnp.concatenate([near, far], axis=1)
        right = jnp.concatenate(
            [
                band_near * jnp.broadcast_to(row[:, :128], (128, 128)),
                band_far * jnp.broadcast_to(row[:, 128:], (128, 128)),
            ],
            axis=1,
        )
        return lax.dot_general(left, right, (((1,), (1,)), ((), ())), preferred_element_type=f32)

    @pl.when(step == 0)
    def _():
        ref32[:rows] = ref_ref[...].astype(f32)
        mate32[:rows] = mate_ref[...].astype(f32)
        ref32[rows:] = jnp.zeros((16, 256), f32)
        mate32[rows:] = jnp.zeros((16, 384), f32)
        k = lax.broadcasted_iota(jnp.int32, (384, 256), 0)
        c = lax.broadcasted_iota(jnp.int32, (384, 256), 1)
        total, total_sq = box_sums(mate_ref[...], ((k - c >= 0) & (k - c <= 8)).astype(bf16))
        for t in range(2):
            mate_sum[t] = total[:, 128 * t : 128 * t + 128]
            mate_sq[t] = total_sq[:, 128 * t : 128 * t + 128]
        k = lax.broadcasted_iota(jnp.int32, (256, 128), 0)
        gap_ref = jnp.where(k < 128, k, k - 112) - lax.broadcasted_iota(jnp.int32, (256, 128), 1)
        weights = ((gap_ref >= 0) & (gap_ref <= 8) & ((k < 128) | (k >= 240))).astype(bf16)
        ref_sum[...], ref_sq[...] = box_sums(ref_ref[...], weights)
        skew(0, 8)
        for r in range(8):
            last_a[r] = one_line(0, r)
        skew(8, 16)
        for r in range(16):
            lines_a[r] = one_line(8, r)

    def copy(block, half, piece):
        size = DISP // PIECES
        return pltpu.make_async_copy(
            sent.at[half, pl.ds(piece * size, size)],
            out_ref.at[pl.ds(piece * size, size), pl.ds(pl.multiple_of(block * RB, RB), RB), :],
            sems.at[half, piece],
        )

    def half_step(half, last_in, lines, last_out, lines_next):
        block = 2 * step + half
        first = pl.multiple_of(block * RB, RB)
        ahead = first + RB + 8

        def window(ref):
            x = [ref[pl.ds(first + i, RB), :] for i in range(9)]
            return ((x[0] + x[1]) + (x[2] + x[3])) + ((x[4] + x[5]) + (x[6] + x[7])) + x[8]

        def inverse(total, total_sq):
            mean = total / 81.0
            return lax.rsqrt(jnp.maximum(total_sq / 81.0 - mean * mean, 0.0) + EPSILON)

        total = window(ref_sum)
        ref_mean, ref_inv = total / 81.0, inverse(total, window(ref_sq))
        m0, m1 = window(mate_sum.at[0]), window(mate_sum.at[1])
        v0 = inverse(m0, window(mate_sq.at[0])) / 81.0
        v1 = inverse(m1, window(mate_sq.at[1])) / 81.0

        @pl.when(step > 0)
        def _():
            for piece in range(PIECES):
                copy(block, half, piece).wait()

        skew(pl.multiple_of(ahead, 8), RB)
        for q in range(16):
            lines_next[q] = one_line(ahead, q)
            h = [last_in[i, 8 * q : 8 * q + 8, :] for i in range(8)]
            h += [lines[i, 8 * q : 8 * q + 8, :] for i in range(RB)]
            for i in range(8):
                last_out[i, 8 * q : 8 * q + 8, :] = h[RB + i]
            for begin in range(0, RB, 9):
                suffix = [None] * 8 + [h[begin + 8]]
                for i in range(7, -1, -1):
                    suffix[i] = h[begin + i] + suffix[i + 1]
                prefix = None
                for i in range(min(9, RB - begin)):
                    total = suffix[i]
                    if i:
                        nxt = h[begin + 8 + i]
                        prefix = nxt if prefix is None else prefix + nxt
                        total = total + prefix
                    sums[pl.ds(8 * q * PITCH + begin + i, 8, stride=PITCH), :] = total
            for k in range(8 * q, 8 * q + 8):
                mean, scale = m0, v0
                if k < 127:
                    keep = lane >= 127 - k
                    mean = pltpu.roll(jnp.where(keep, m0, m1), k + 1, axis=1)
                    scale = pltpu.roll(jnp.where(keep, v0, v1), k + 1, axis=1)
                value = (sums[pl.ds(k * PITCH, RB), :] - ref_mean * mean) * ref_inv * scale
                sent[half, k] = value.astype(bf16)
            if (q + 1) % (16 // PIECES) == 0:
                copy(block, half, q // (16 // PIECES)).start()

    half_step(0, last_a, lines_a, last_b, lines_b)
    half_step(1, last_b, lines_b, last_a, lines_a)

    @pl.when(step == pl.num_programs(0) - 1)
    def _():
        for half in range(2):
            for piece in range(PIECES):
                copy(0, half, piece).wait()


def cost(ref_rows, mate_rows):
    rows = ref_rows.shape[0]
    f32 = jnp.float32
    vmem = pl.BlockSpec(memory_space=pltpu.VMEM)
    return pl.pallas_call(
        cost_kernel,
        out_shape=jax.ShapeDtypeStruct((DISP, rows - 8, COLS), jnp.bfloat16),
        grid=((rows - 8) // (2 * RB),),
        in_specs=[vmem, vmem],
        out_specs=pl.BlockSpec(memory_space=pl.ANY),
        scratch_shapes=[
            pltpu.VMEM((rows + 16, 256), f32),
            pltpu.VMEM((rows + 16, 384), f32),
            pltpu.VMEM((3, 16 * PITCH + 8, 128), f32),
            pltpu.VMEM((RB, 128, 128), f32),
            pltpu.VMEM((RB, 128, 128), f32),
            pltpu.VMEM((8, 128, 128), f32),
            pltpu.VMEM((8, 128, 128), f32),
            pltpu.VMEM((128 * PITCH + 8, 128), f32),
            pltpu.VMEM((2, DISP, RB, COLS), jnp.bfloat16),
            pltpu.SemaphoreType.DMA((2, PIECES)),
            pltpu.VMEM((2, rows, 128), f32),
            pltpu.VMEM((2, rows, 128), f32),
            pltpu.VMEM((rows, 128), f32),
            pltpu.VMEM((rows, 128), f32),
        ],
        compiler_params=pltpu.CompilerParams(dimension_semantics=("arbitrary",), vmem_limit_bytes=40 << 20),
        name="cost_volume",
    )(ref_rows, mate_rows)


SPAN = COLS + DISP + 8
EDGE = 4
REF_FROM = OFF_MAX + DISP - 1


def slot_count(rows_dev, strips):
    wide = rows_dev // strips + 2 * EDGE
    return -(-wide // 8) * 8


def places(ids, low, rows_dev):
    line = ids.shape[1]
    place = ids - low + EDGE
    wanted = (place >= 0) & (place < rows_dev + 2 * EDGE)
    before = lax.broadcasted_iota(jnp.int32, (line, line), 0)
    after = lax.broadcasted_iota(jnp.int32, (line, line), 1)
    earlier = (before < after).astype(jnp.bfloat16)
    flags = jnp.where(wanted, 1.0, 0.0)
    pad = (-flags.shape[0]) % 16
    if pad:
        flags = jnp.concatenate([flags, jnp.zeros((pad, line), jnp.float32)], axis=0)
    rank = jnp.dot(flags.astype(jnp.bfloat16), earlier, preferred_element_type=jnp.float32)
    rank = rank[: ids.shape[0]].astype(jnp.int32)
    return jnp.where(wanted, rank, -1), place


def spread(rank, slots):
    strips, line = rank.shape
    wide = jnp.broadcast_to(rank[:, None, :], (strips, slots, line))
    return wide == lax.broadcasted_iota(jnp.int32, (strips, slots, line), 1)


def pack_kernel(map_ref, tiles_ref, out_ref):
    strips, slots, width = out_ref.shape
    rows_dev = tiles_ref.shape[0]
    ids = jnp.broadcast_to(map_ref[pl.ds(lax.axis_index("strip"), 1), :], (strips, rows_dev))
    low = rows_dev * lax.broadcasted_iota(jnp.int32, (strips, rows_dev), 0)
    rank, _ = places(ids, low, rows_dev)
    pick = jnp.where(spread(rank, slots), 1.0, 0.0).reshape(strips * slots, rows_dev).astype(jnp.bfloat16)
    rows = jnp.dot(pick, tiles_ref[...], preferred_element_type=jnp.float32)
    out_ref[...] = rows.astype(jnp.bfloat16).reshape(out_ref.shape)


def table_kernel(table_ref, out_ref):
    strips, rows_dev = table_ref.shape
    rows, positions = out_ref.shape
    slots = positions // strips
    low = rows_dev * lax.axis_index("strip")
    rank, place = places(table_ref[...], low, rows_dev)
    wide = jnp.broadcast_to(place[:, None, :], (strips, slots, rows_dev))
    named = jnp.where(spread(rank, slots), wide + 1, 0).astype(jnp.float32)
    named = named.reshape(positions, rows_dev).astype(jnp.bfloat16)
    ones = jnp.ones((16, rows_dev), jnp.bfloat16)
    target = lax.dot_general(ones, named, (((1,), (1,)), ((), ())), preferred_element_type=jnp.float32)
    target = jnp.broadcast_to(target[:1].astype(jnp.int32), (rows, positions))
    mine = lax.broadcasted_iota(jnp.int32, (rows, positions), 0) + 1
    out_ref[...] = jnp.where(target == mine, 1.0, 0.0).astype(jnp.bfloat16)


def unpack_kernel(offsets_ref, step_ref, table_ref, arrived_ref, ref_ref, slab_ref, strip):
    rows = ref_ref.shape[0]
    width = arrived_ref.shape[1]
    views = offsets_ref.shape[0]
    own = jnp.dot(table_ref[...], arrived_ref[...], preferred_element_type=jnp.float32)
    strip[:, :width] = own
    strip[:, width:] = jnp.zeros((rows, strip.shape[1] - width), jnp.float32)
    ref_ref[:, :128] = own[:, REF_FROM : REF_FROM + 128].astype(jnp.bfloat16)
    ref_ref[:, 128:] = strip[:, REF_FROM + 16 : REF_FROM + 144].astype(jnp.bfloat16)
    receiver = lax.rem(lax.axis_index("view") + views - lax.rem(step_ref[0], views), views)
    start = jnp.clip(OFF_MAX - offsets_ref[receiver, 0], 0, OFF_MAX)
    whole = start // 128
    part = start - whole * 128
    block = strip[:, pl.ds(pl.multiple_of(whole * 128, 128), 512)]
    turned = pltpu.roll(block, 512 - part, axis=1)
    slab_ref[...] = turned[:, :384].astype(jnp.bfloat16)


def shards(images, offsets, pair_step, row_map):
    own_tiles = images[0]
    rows_dev, width = own_tiles.shape
    strips = lax.axis_size("strip")
    views = lax.axis_size("view")
    slots = slot_count(rows_dev, strips)
    rows = rows_dev + 2 * EDGE
    bf16 = jnp.bfloat16
    table = row_map.reshape(strips, rows_dev)
    outgoing = pl.pallas_call(
        pack_kernel, out_shape=jax.ShapeDtypeStruct((strips, slots, width), bf16), name="pack"
    )(table, own_tiles)
    arrived = lax.all_to_all(outgoing, "strip", split_axis=0, concat_axis=0, tiled=True)
    select = pl.pallas_call(
        table_kernel, out_shape=jax.ShapeDtypeStruct((rows, strips * slots), bf16), name="table"
    )(table)
    smem = pl.BlockSpec(memory_space=pltpu.SMEM)
    vmem = pl.BlockSpec(memory_space=pltpu.VMEM)
    ref_rows, slab = pl.pallas_call(
        unpack_kernel,
        out_shape=(jax.ShapeDtypeStruct((rows, 256), bf16), jax.ShapeDtypeStruct((rows, 384), bf16)),
        in_specs=[smem, smem, vmem, vmem],
        scratch_shapes=[pltpu.VMEM((rows, 768), jnp.float32)],
        name="unpack",
    )(offsets, pair_step, select, arrived.reshape(strips * slots, width))

    def sent_by(step):
        return lambda rows_out: lax.ppermute(rows_out, "view", [(i, (i - step) % views) for i in range(views)])

    mate_rows = lax.switch(pair_step[0] % views - 1, [sent_by(step) for step in range(1, views)], slab)
    return cost(ref_rows, mate_rows)[None]


def solution(mesh):
    in_specs = (P("view", "strip", None), P(None, "strip"), P("strip"), P())
    out_specs = P("view", None, "strip", None)
    return jax.shard_map(shards, mesh=mesh, in_specs=in_specs, out_specs=out_specs, check_vma=False)
```

```python
import functools

import jax
import jax.numpy as jnp
from jax import lax
from jax.experimental import pallas as pl
from jax.experimental.pallas import tpu as pltpu
from jax.sharding import PartitionSpec as P

COLS = 128
DISP = 128
OFF_MAX = 376


EPSILON = 1e-05


RB = 16
PITCH = 17
PIECES = 2


def box_sums(values, weights):
    f32, bf16 = jnp.float32, jnp.bfloat16
    wide = values.astype(f32)
    square = wide * wide
    high = square.astype(bf16)
    low = (square - high.astype(f32)).astype(bf16)
    total = jnp.dot(values, weights, preferred_element_type=f32)
    total_sq = jnp.dot(high, weights, preferred_element_type=f32)
    return total, total_sq + jnp.dot(low, weights, preferred_element_type=f32)


def cost_kernel(ref_ref, mate_ref, out_ref, ref32, mate32, base_a, base_b, lines_a, lines_b, last_a, last_b, sums_a, sums_b, sent, sems,
                mate_sum, mate_sq, ref_sum, ref_sq, stats):
    step = pl.program_id(0)
    rows = ref_ref.shape[0]
    f32, bf16 = jnp.float32, jnp.bfloat16
    down = lax.broadcasted_iota(jnp.int32, (128, 128), 0)
    across = lax.broadcasted_iota(jnp.int32, (128, 128), 1)
    gap = across - down
    band_near = ((gap >= 0) & (gap <= 8)).astype(bf16)
    band_far = ((gap >= -16) & (gap <= -8) & (across >= 112)).astype(bf16)[112:]
    lane = lax.broadcasted_iota(jnp.int32, (8, 128), 1)
    lane_two = lax.broadcasted_iota(jnp.int32, (16, 128), 1)

    def skew(base, block, s):
        shift = 15 - s
        for t in range(2):
            part = block[t]
            if shift:
                part = pltpu.roll(jnp.where(lane_two < shift, block[t + 1], part), 128 - shift, axis=1)
            part = part.astype(f32)
            for r in range(0, RB, 8):
                base[t, pl.ds(r * PITCH + s, 8, stride=PITCH), :] = part[r : r + 8]

    def lines_from(first):
        block = mate32[pl.ds(first, RB), :].astype(bf16)
        return [block[:, 128 * t : 128 * t + 128] for t in range(3)]

    def one_line(base, first, r):
        tiles = [base[t, pl.ds(r * PITCH, 16), :].astype(bf16) for t in range(2)]
        parts = []
        for p in range(-1, 8):
            shift = 112 - 16 * p
            if shift in (0, 128):
                part = tiles[shift // 128]
            else:
                part = pltpu.roll(jnp.where(lane_two < shift, tiles[1], tiles[0]), 128 - shift, axis=1)
            parts.append(part)
        near = jnp.concatenate(parts[1:], axis=0)
        far = jnp.concatenate(parts[:-1], axis=0)
        row = ref32[pl.ds(first + r, 1), :].astype(bf16)
        left = jnp.concatenate([near, far], axis=1)
        beyond = jnp.concatenate(
            [jnp.zeros((112, 128), bf16), band_far * jnp.broadcast_to(row[:, 128:], (16, 128))], axis=0
        )
        right = jnp.concatenate([band_near * jnp.broadcast_to(row[:, :128], (128, 128)), beyond], axis=1)
        return lax.dot_general(left, right, (((1,), (1,)), ((), ())), preferred_element_type=f32)

    @pl.when(step == 0)
    def _():
        ref32[:rows] = ref_ref[...].astype(f32)
        mate32[:rows] = mate_ref[...].astype(f32)
        ref32[rows:] = jnp.zeros((16, 256), f32)
        mate32[rows:] = jnp.zeros((32, 384), f32)
        k = lax.broadcasted_iota(jnp.int32, (384, 256), 0)
        c = lax.broadcasted_iota(jnp.int32, (384, 256), 1)
        total, total_sq = box_sums(mate_ref[...], ((k - c >= 0) & (k - c <= 8)).astype(bf16))
        for t in range(2):
            mate_sum[t] = total[:, 128 * t : 128 * t + 128]
            mate_sq[t] = total_sq[:, 128 * t : 128 * t + 128]
        k = lax.broadcasted_iota(jnp.int32, (256, 128), 0)
        gap_ref = jnp.where(k < 128, k, k - 112) - lax.broadcasted_iota(jnp.int32, (256, 128), 1)
        weights = ((gap_ref >= 0) & (gap_ref <= 8) & ((k < 128) | (k >= 240))).astype(bf16)
        ref_sum[...], ref_sq[...] = box_sums(ref_ref[...], weights)
        for base, first in ((base_b, 0), (base_a, 8)):
            block = lines_from(first)
            for s in range(16):
                skew(base, block, s)
        for r in range(8):
            last_a[r] = one_line(base_b, 0, r)
        for r in range(16):
            lines_a[r] = one_line(base_a, 8, r)
        block = lines_from(24)
        for s in range(16):
            skew(base_b, block, s)

        def window(ref):
            x = [ref[i : i + rows - 8, :] for i in range(9)]
            return ((x[0] + x[1]) + (x[2] + x[3])) + ((x[4] + x[5]) + (x[6] + x[7])) + x[8]

        def inverse(total, total_sq):
            mean = total / 81.0
            return lax.rsqrt(jnp.maximum(total_sq / 81.0 - mean * mean, 0.0) + EPSILON)

        for t in range(2):
            total = window(mate_sum.at[t])
            stats[t] = total
            stats[2 + t] = inverse(total, window(mate_sq.at[t])) / 81.0
        total = window(ref_sum)
        stats[4] = total / 81.0
        stats[5] = inverse(total, window(ref_sq))

    def copy(block, half, piece):
        size = DISP // PIECES
        return pltpu.make_async_copy(
            sent.at[half, pl.ds(piece * size, size)],
            out_ref.at[pl.ds(piece * size, size), pl.ds(pl.multiple_of(block * RB, RB), RB), :],
            sems.at[half, piece],
        )

    def half_step(half, last_in, lines, last_out, lines_next, base, base_next):
        block = 2 * step + half
        first = pl.multiple_of(block * RB, RB)
        ahead = first + RB + 8

        @pl.when(step > 0)
        def _():
            for piece in range(PIECES):
                copy(block, half, piece).wait()

        block_next = lines_from(pl.multiple_of(ahead + RB, 8))

        def vertical(q, sums):
            h = [last_in[i, 8 * q : 8 * q + 8, :] for i in range(8)]
            h += [lines[i, 8 * q : 8 * q + 8, :] for i in range(RB)]
            for i in range(8):
                last_out[i, 8 * q : 8 * q + 8, :] = h[RB + i]
            for begin in range(0, RB, 9):
                suffix = [None] * 8 + [h[begin + 8]]
                for i in range(7, -1, -1):
                    suffix[i] = h[begin + i] + suffix[i + 1]
                prefix = None
                for i in range(min(9, RB - begin)):
                    total = suffix[i]
                    if i:
                        nxt = h[begin + 8 + i]
                        prefix = nxt if prefix is None else prefix + nxt
                        total = total + prefix
                    sums[pl.ds(begin + i, 8, stride=PITCH), :] = total

        def normalize(q, sums):
            for j in range(8):
                k = 8 * q + j
                done = []
                for u in range(0, RB, 8):
                    m0, m1, v0, v1, ref_mean, ref_inv = [
                        stats[i, pl.ds(pl.multiple_of(first + u, 8), 8), :] for i in range(6)
                    ]
                    mean, scale = m0, v0
                    if k < 127:
                        mean = pltpu.roll(jnp.where(lane >= 127 - k, m0, m1), k + 1, axis=1)
                        scale = pltpu.roll(jnp.where(lane >= 127 - k, v0, v1), k + 1, axis=1)
                    total = sums[pl.ds(j * PITCH + u, 8), :]
                    done.append((total - ref_mean * mean) * ref_inv * scale)
                sent[half, k] = jnp.concatenate(done, axis=0).astype(bf16)
            if (q + 1) % (16 // PIECES) == 0:
                copy(block, half, q // (16 // PIECES)).start()

        both = (sums_a, sums_b)
        for q in range(16):
            lines_next[q] = one_line(base, ahead, q)
            skew(base_next, block_next, q)
            vertical(q, both[q % 2])
            if q:
                normalize(q - 1, both[(q - 1) % 2])
        normalize(15, both[1])

    half_step(0, last_a, lines_a, last_b, lines_b, base_b, base_a)
    half_step(1, last_b, lines_b, last_a, lines_a, base_a, base_b)

    @pl.when(step == pl.num_programs(0) - 1)
    def _():
        for half in range(2):
            for piece in range(PIECES):
                copy(0, half, piece).wait()


def cost(ref_rows, mate_rows):
    rows = ref_rows.shape[0]
    f32 = jnp.float32
    vmem = pl.BlockSpec(memory_space=pltpu.VMEM)
    return pl.pallas_call(
        cost_kernel,
        out_shape=jax.ShapeDtypeStruct((DISP, rows - 8, COLS), jnp.bfloat16),
        grid=((rows - 8) // (2 * RB),),
        in_specs=[vmem, vmem],
        out_specs=pl.BlockSpec(memory_space=pl.ANY),
        scratch_shapes=[
            pltpu.VMEM((rows + 16, 256), f32),
            pltpu.VMEM((rows + 32, 384), f32),
            pltpu.VMEM((2, 16 * PITCH + 8, 128), f32),
            pltpu.VMEM((2, 16 * PITCH + 8, 128), f32),
            pltpu.VMEM((RB, 128, 128), f32),
            pltpu.VMEM((RB, 128, 128), f32),
            pltpu.VMEM((8, 128, 128), f32),
            pltpu.VMEM((8, 128, 128), f32),
            pltpu.VMEM((8 * PITCH + 8, 128), f32),
            pltpu.VMEM((8 * PITCH + 8, 128), f32),
            pltpu.VMEM((2, DISP, RB, COLS), jnp.bfloat16),
            pltpu.SemaphoreType.DMA((2, PIECES)),
            pltpu.VMEM((2, rows, 128), f32),
            pltpu.VMEM((2, rows, 128), f32),
            pltpu.VMEM((rows, 128), f32),
            pltpu.VMEM((rows, 128), f32),
            pltpu.VMEM((6, rows - 8, 128), f32),
        ],
        compiler_params=pltpu.CompilerParams(dimension_semantics=("arbitrary",), vmem_limit_bytes=16 << 20),
        name="cost_volume",
    )(ref_rows, mate_rows)


SPAN = COLS + DISP + 8
EDGE = 4
SMALL = pltpu.CompilerParams(vmem_limit_bytes=16 << 20)
REF_FROM = OFF_MAX + DISP - 1


def slot_count(rows_dev, strips):
    wide = rows_dev // strips + 2 * EDGE
    return -(-wide // 8) * 8


def places(ids, low, rows_dev):
    line = ids.shape[1]
    place = ids - low + EDGE
    wanted = (place >= 0) & (place < rows_dev + 2 * EDGE)
    before = lax.broadcasted_iota(jnp.int32, (line, line), 0)
    after = lax.broadcasted_iota(jnp.int32, (line, line), 1)
    earlier = (before < after).astype(jnp.bfloat16)
    flags = jnp.where(wanted, 1.0, 0.0)
    pad = (-flags.shape[0]) % 16
    if pad:
        flags = jnp.concatenate([flags, jnp.zeros((pad, line), jnp.float32)], axis=0)
    rank = jnp.dot(flags.astype(jnp.bfloat16), earlier, preferred_element_type=jnp.float32)
    rank = rank[: ids.shape[0]].astype(jnp.int32)
    return jnp.where(wanted, rank, -1), place


def spread(rank, slots):
    strips, line = rank.shape
    wide = jnp.broadcast_to(rank[:, None, :], (strips, slots, line))
    return wide == lax.broadcasted_iota(jnp.int32, (strips, slots, line), 1)


def pack_kernel(map_ref, tiles_ref, out_ref):
    strips, slots, width = out_ref.shape
    rows_dev = tiles_ref.shape[0]
    ids = jnp.broadcast_to(map_ref[pl.ds(lax.axis_index("strip"), 1), :], (strips, rows_dev))
    low = rows_dev * lax.broadcasted_iota(jnp.int32, (strips, rows_dev), 0)
    rank, _ = places(ids, low, rows_dev)
    pick = jnp.where(spread(rank, slots), 1.0, 0.0).reshape(strips * slots, rows_dev).astype(jnp.bfloat16)
    rows = jnp.dot(pick, tiles_ref[...], preferred_element_type=jnp.float32)
    out_ref[...] = rows.astype(jnp.bfloat16).reshape(out_ref.shape)


def table_kernel(table_ref, out_ref):
    strips, rows_dev = table_ref.shape
    rows, positions = out_ref.shape
    slots = positions // strips
    low = rows_dev * lax.axis_index("strip")
    rank, place = places(table_ref[...], low, rows_dev)
    wide = jnp.broadcast_to(place[:, None, :], (strips, slots, rows_dev))
    named = jnp.where(spread(rank, slots), wide + 1, 0).astype(jnp.float32)
    named = named.reshape(positions, rows_dev).astype(jnp.bfloat16)
    ones = jnp.ones((16, rows_dev), jnp.bfloat16)
    target = lax.dot_general(ones, named, (((1,), (1,)), ((), ())), preferred_element_type=jnp.float32)
    target = jnp.broadcast_to(target[:1].astype(jnp.int32), (rows, positions))
    mine = lax.broadcasted_iota(jnp.int32, (rows, positions), 0) + 1
    out_ref[...] = jnp.where(target == mine, 1.0, 0.0).astype(jnp.bfloat16)


def unpack_kernel(offsets_ref, step_ref, table_ref, arrived_ref, ref_ref, slab_ref, strip):
    rows = ref_ref.shape[0]
    width = arrived_ref.shape[1]
    views = offsets_ref.shape[0]
    own = jnp.dot(table_ref[...], arrived_ref[...], preferred_element_type=jnp.float32)
    strip[:, :width] = own
    strip[:, width:] = jnp.zeros((rows, strip.shape[1] - width), jnp.float32)
    ref_ref[:, :128] = own[:, REF_FROM : REF_FROM + 128].astype(jnp.bfloat16)
    ref_ref[:, 128:] = strip[:, REF_FROM + 16 : REF_FROM + 144].astype(jnp.bfloat16)
    receiver = lax.rem(lax.axis_index("view") + views - lax.rem(step_ref[0], views), views)
    start = jnp.clip(OFF_MAX - offsets_ref[receiver, 0], 0, OFF_MAX)
    whole = start // 128
    part = start - whole * 128
    block = strip[:, pl.ds(pl.multiple_of(whole * 128, 128), 512)]
    turned = pltpu.roll(block, 512 - part, axis=1)
    slab_ref[...] = turned[:, :384].astype(jnp.bfloat16)


def shards(images, offsets, pair_step, row_map):
    own_tiles = images[0]
    rows_dev, width = own_tiles.shape
    strips = lax.axis_size("strip")
    views = lax.axis_size("view")
    slots = slot_count(rows_dev, strips)
    rows = rows_dev + 2 * EDGE
    bf16 = jnp.bfloat16
    table = row_map.reshape(strips, rows_dev)
    outgoing = pl.pallas_call(
        pack_kernel, out_shape=jax.ShapeDtypeStruct((strips, slots, width), bf16), name="pack"
    )(table, own_tiles)
    arrived = lax.all_to_all(outgoing, "strip", split_axis=0, concat_axis=0, tiled=True)
    select = pl.pallas_call(
        table_kernel, out_shape=jax.ShapeDtypeStruct((rows, strips * slots), bf16), name="table", compiler_params=SMALL
    )(table)
    smem = pl.BlockSpec(memory_space=pltpu.SMEM)
    vmem = pl.BlockSpec(memory_space=pltpu.VMEM)
    ref_rows, slab = pl.pallas_call(
        unpack_kernel,
        out_shape=(jax.ShapeDtypeStruct((rows, 256), bf16), jax.ShapeDtypeStruct((rows, 384), bf16)),
        in_specs=[smem, smem, vmem, vmem],
        scratch_shapes=[pltpu.VMEM((rows, 768), jnp.float32)],
        compiler_params=SMALL,
        name="unpack",
    )(offsets, pair_step, select, arrived.reshape(strips * slots, width))

    def sent_by(step):
        return lambda rows_out: lax.ppermute(rows_out, "view", [(i, (i - step) % views) for i in range(views)])

    mate_rows = lax.switch(pair_step[0] % views - 1, [sent_by(step) for step in range(1, views)], slab)
    return cost(ref_rows, mate_rows)[None]


def solution(mesh):
    in_specs = (P("view", "strip", None), P(None, "strip"), P("strip"), P())
    out_specs = P("view", None, "strip", None)
    return jax.shard_map(shards, mesh=mesh, in_specs=in_specs, out_specs=out_specs, check_vma=False)
```

```python
import functools

import jax
import jax.numpy as jnp
from jax import lax
from jax.experimental import pallas as pl
from jax.experimental.pallas import tpu as pltpu
from jax.sharding import PartitionSpec as P

COLS = 128
DISP = 128
OFF_MAX = 376


EPSILON = 1e-05


RB = 16
PITCH = 17
PIECES = 2


def box_sums(values, weights):
    bf16 = jnp.bfloat16
    rows = values.shape[0]
    square = values * values
    high = square.astype(bf16).astype(jnp.float32)
    lines = jnp.concatenate([values, high, square - high], axis=0).astype(bf16)
    sums = jnp.dot(lines, weights, preferred_element_type=jnp.float32)
    return sums[:rows], sums[rows : 2 * rows] + sums[2 * rows :]


def cost_kernel(ref_ref, mate_ref, out_ref, ref32, mate32, base_a, base_b, lines_a, lines_b, last_a, last_b, sums_a, sums_b, sent, sems,
                mate_sum, mate_sq, ref_sum, ref_sq, stats, mate_here, mate_sem):
    step = pl.program_id(0)
    rows = ref_ref.shape[0]
    f32, bf16 = jnp.float32, jnp.bfloat16
    down = lax.broadcasted_iota(jnp.int32, (128, 128), 0)
    across = lax.broadcasted_iota(jnp.int32, (128, 128), 1)
    gap = across - down
    band_near = ((gap >= 0) & (gap <= 8)).astype(bf16)
    band_far = ((gap >= -16) & (gap <= -8) & (across >= 112)).astype(bf16)[112:]
    lane = lax.broadcasted_iota(jnp.int32, (8, 128), 1)
    lane_two = lax.broadcasted_iota(jnp.int32, (16, 128), 1)

    def skew(base, block, s):
        shift = 15 - s
        for t in range(2):
            part = block[t]
            if shift:
                part = pltpu.roll(jnp.where(lane_two < shift, block[t + 1], part), 128 - shift, axis=1)
            part = part.astype(f32)
            for r in range(0, RB, 8):
                base[t, pl.ds(r * PITCH + s, 8, stride=PITCH), :] = part[r : r + 8]

    def lines_from(first):
        block = mate32[pl.ds(first, RB), :].astype(bf16)
        return [block[:, 128 * t : 128 * t + 128] for t in range(3)]

    def one_line(base, first, r):
        tiles = [base[t, pl.ds(r * PITCH, 16), :].astype(bf16) for t in range(2)]
        parts = []
        for p in range(-1, 8):
            shift = 112 - 16 * p
            if shift in (0, 128):
                part = tiles[shift // 128]
            else:
                part = pltpu.roll(jnp.where(lane_two < shift, tiles[1], tiles[0]), 128 - shift, axis=1)
            parts.append(part)
        near = jnp.concatenate(parts[1:], axis=0)
        far = jnp.concatenate(parts[:-1], axis=0)
        row = ref32[pl.ds(first + r, 1), :].astype(bf16)
        left = jnp.concatenate([near, far], axis=1)
        beyond = jnp.concatenate(
            [jnp.zeros((112, 128), bf16), band_far * jnp.broadcast_to(row[:, 128:], (16, 128))], axis=0
        )
        right = jnp.concatenate([band_near * jnp.broadcast_to(row[:, :128], (128, 128)), beyond], axis=1)
        return lax.dot_general(left, right, (((1,), (1,)), ((), ())), preferred_element_type=f32)

    @pl.when(step == 0)
    def _():
        arrival = pltpu.make_async_copy(mate_ref, mate_here, mate_sem)
        arrival.start()

        def window(ref):
            x = [ref[i : i + rows - 8, :] for i in range(9)]
            return ((x[0] + x[1]) + (x[2] + x[3])) + ((x[4] + x[5]) + (x[6] + x[7])) + x[8]

        def inverse(total, total_sq):
            mean = total / 81.0
            return lax.rsqrt(jnp.maximum(total_sq / 81.0 - mean * mean, 0.0) + EPSILON)

        ref32[:rows] = ref_ref[...].astype(f32)
        ref32[rows:] = jnp.zeros((16, 256), f32)
        mate32[rows:] = jnp.zeros((32, 384), f32)
        k = lax.broadcasted_iota(jnp.int32, (256, 128), 0)
        gap_ref = jnp.where(k < 128, k, k - 112) - lax.broadcasted_iota(jnp.int32, (256, 128), 1)
        weights = ((gap_ref >= 0) & (gap_ref <= 8) & ((k < 128) | (k >= 240))).astype(bf16)
        ref_sum[...], ref_sq[...] = box_sums(ref32[:rows], weights)
        total = window(ref_sum)
        stats[4] = total / 81.0
        stats[5] = inverse(total, window(ref_sq))
        k = lax.broadcasted_iota(jnp.int32, (256, 256), 0)
        c = lax.broadcasted_iota(jnp.int32, (256, 256), 1)
        weights = ((k - c >= 0) & (k - c <= 8)).astype(bf16)
        k, c = k[:16] + 256, c[:16]
        beyond = jnp.where((k - c >= 0) & (k - c <= 8), 1.0, 0.0)
        beyond = jnp.concatenate([beyond, jnp.zeros((112, 256), f32)], axis=0).astype(bf16)
        weights = jnp.concatenate([weights, beyond], axis=0)
        same = lax.broadcasted_iota(jnp.int32, (rows, 256), 0) == lax.broadcasted_iota(jnp.int32, (rows, 256), 1)
        same = same.astype(bf16)
        arrival.wait()
        held = mate_here[...].astype(f32)
        rest = jnp.concatenate([held[rows:], jnp.zeros((120, 256), f32)], axis=0).astype(bf16)
        mate32[:rows, :256] = held[:rows]
        mate32[:rows, 256:] = lax.dot_general(same, rest, (((1,), (1,)), ((), ())), preferred_element_type=f32)
        total, total_sq = box_sums(mate32[:rows], weights)
        for t in range(2):
            mate_sum[t] = total[:, 128 * t : 128 * t + 128]
            mate_sq[t] = total_sq[:, 128 * t : 128 * t + 128]
        for base, first in ((base_b, 0), (base_a, 8)):
            block = lines_from(first)
            for s in range(16):
                skew(base, block, s)
        for r in range(8):
            last_a[r] = one_line(base_b, 0, r)
        for r in range(16):
            lines_a[r] = one_line(base_a, 8, r)
        block = lines_from(24)
        for s in range(16):
            skew(base_b, block, s)

        for t in range(2):
            total = window(mate_sum.at[t])
            stats[t] = total
            stats[2 + t] = inverse(total, window(mate_sq.at[t])) / 81.0

    def copy(block, half, piece):
        size = DISP // PIECES
        return pltpu.make_async_copy(
            sent.at[half, pl.ds(piece * size, size)],
            out_ref.at[pl.ds(piece * size, size), pl.ds(pl.multiple_of(block * RB, RB), RB), :],
            sems.at[half, piece],
        )

    def half_step(half, last_in, lines, last_out, lines_next, base, base_next):
        block = 2 * step + half
        first = pl.multiple_of(block * RB, RB)
        ahead = first + RB + 8

        @pl.when(step > 0)
        def _():
            for piece in range(PIECES):
                copy(block, half, piece).wait()

        block_next = lines_from(pl.multiple_of(ahead + RB, 8))

        def vertical(q, sums):
            h = [last_in[i, 8 * q : 8 * q + 8, :] for i in range(8)]
            h += [lines[i, 8 * q : 8 * q + 8, :] for i in range(RB)]
            for i in range(8):
                last_out[i, 8 * q : 8 * q + 8, :] = h[RB + i]
            for begin in range(0, RB, 9):
                suffix = [None] * 8 + [h[begin + 8]]
                for i in range(7, -1, -1):
                    suffix[i] = h[begin + i] + suffix[i + 1]
                prefix = None
                for i in range(min(9, RB - begin)):
                    total = suffix[i]
                    if i:
                        nxt = h[begin + 8 + i]
                        prefix = nxt if prefix is None else prefix + nxt
                        total = total + prefix
                    sums[pl.ds(begin + i, 8, stride=PITCH), :] = total

        def normalize(q, sums):
            for j in range(8):
                k = 8 * q + j
                done = []
                for u in range(0, RB, 8):
                    m0, m1, v0, v1, ref_mean, ref_inv = [
                        stats[i, pl.ds(pl.multiple_of(first + u, 8), 8), :] for i in range(6)
                    ]
                    mean, scale = m0, v0
                    if k < 127:
                        mean = pltpu.roll(jnp.where(lane >= 127 - k, m0, m1), k + 1, axis=1)
                        scale = pltpu.roll(jnp.where(lane >= 127 - k, v0, v1), k + 1, axis=1)
                    total = sums[pl.ds(j * PITCH + u, 8), :]
                    done.append((total - ref_mean * mean) * ref_inv * scale)
                sent[half, k] = jnp.concatenate(done, axis=0).astype(bf16)
            if (q + 1) % (16 // PIECES) == 0:
                copy(block, half, q // (16 // PIECES)).start()

        both = (sums_a, sums_b)
        for q in range(16):
            lines_next[q] = one_line(base, ahead, q)
            skew(base_next, block_next, q)
            vertical(q, both[q % 2])
            if q:
                normalize(q - 1, both[(q - 1) % 2])
        normalize(15, both[1])

    half_step(0, last_a, lines_a, last_b, lines_b, base_b, base_a)
    half_step(1, last_b, lines_b, last_a, lines_a, base_a, base_b)

    @pl.when(step == pl.num_programs(0) - 1)
    def _():
        for half in range(2):
            for piece in range(PIECES):
                copy(0, half, piece).wait()


def cost(ref_rows, mate_rows):
    rows = ref_rows.shape[0]
    f32 = jnp.float32
    vmem = pl.BlockSpec(memory_space=pltpu.VMEM)
    return pl.pallas_call(
        cost_kernel,
        out_shape=jax.ShapeDtypeStruct((DISP, rows - 8, COLS), jnp.bfloat16),
        grid=((rows - 8) // (2 * RB),),
        in_specs=[vmem, pl.BlockSpec(memory_space=pl.ANY)],
        out_specs=pl.BlockSpec(memory_space=pl.ANY),
        scratch_shapes=[
            pltpu.VMEM((rows + 16, 256), f32),
            pltpu.VMEM((rows + 32, 384), f32),
            pltpu.VMEM((2, 16 * PITCH + 8, 128), f32),
            pltpu.VMEM((2, 16 * PITCH + 8, 128), f32),
            pltpu.VMEM((RB, 128, 128), f32),
            pltpu.VMEM((RB, 128, 128), f32),
            pltpu.VMEM((8, 128, 128), f32),
            pltpu.VMEM((8, 128, 128), f32),
            pltpu.VMEM((8 * PITCH + 8, 128), f32),
            pltpu.VMEM((8 * PITCH + 8, 128), f32),
            pltpu.VMEM((2, DISP, RB, COLS), jnp.bfloat16),
            pltpu.SemaphoreType.DMA((2, PIECES)),
            pltpu.VMEM((2, rows, 128), f32),
            pltpu.VMEM((2, rows, 128), f32),
            pltpu.VMEM((rows, 128), f32),
            pltpu.VMEM((rows, 128), f32),
            pltpu.VMEM((6, rows - 8, 128), f32),
            pltpu.VMEM(mate_rows.shape, mate_rows.dtype),
            pltpu.SemaphoreType.DMA,
        ],
        compiler_params=pltpu.CompilerParams(dimension_semantics=("arbitrary",), vmem_limit_bytes=16 << 20),
        name="cost_volume",
    )(ref_rows, mate_rows)


SPAN = COLS + DISP + 8
EDGE = 4
PARTS = 4
SMALL = pltpu.CompilerParams(vmem_limit_bytes=16 << 20)
REF_FROM = OFF_MAX + DISP - 1


def slot_count(rows_dev, strips):
    wide = rows_dev // strips + 2 * EDGE
    return -(-wide // 8) * 8


def places(ids, low, rows_dev):
    line = ids.shape[1]
    place = ids - low + EDGE
    wanted = (place >= 0) & (place < rows_dev + 2 * EDGE)
    before = lax.broadcasted_iota(jnp.int32, (line, line), 0)
    after = lax.broadcasted_iota(jnp.int32, (line, line), 1)
    earlier = (before < after).astype(jnp.bfloat16)
    flags = jnp.where(wanted, 1.0, 0.0)
    pad = (-flags.shape[0]) % 16
    if pad:
        flags = jnp.concatenate([flags, jnp.zeros((pad, line), jnp.float32)], axis=0)
    rank = jnp.dot(flags.astype(jnp.bfloat16), earlier, preferred_element_type=jnp.float32)
    rank = rank[: ids.shape[0]].astype(jnp.int32)
    return jnp.where(wanted, rank, -1), place


def spread(rank, slots):
    strips, line = rank.shape
    wide = jnp.broadcast_to(rank[:, None, :], (strips, slots, line))
    return wide == lax.broadcasted_iota(jnp.int32, (strips, slots, line), 1)


def pack_kernel(map_ref, tiles_ref, out_ref, map_here, tiles_here, out_here, sems):
    strips, slots, width = out_ref.shape
    rows_dev = tiles_ref.shape[0]
    map_copy = pltpu.make_async_copy(map_ref, map_here, sems.at[0])
    tiles_copy = pltpu.make_async_copy(tiles_ref, tiles_here, sems.at[1])
    map_copy.start()
    tiles_copy.start()
    map_copy.wait()
    ids = jnp.broadcast_to(map_here[pl.ds(lax.axis_index("strip"), 1), :], (strips, rows_dev))
    low = rows_dev * lax.broadcasted_iota(jnp.int32, (strips, rows_dev), 0)
    rank, _ = places(ids, low, rows_dev)
    share = strips // PARTS
    picks = []
    for part in range(PARTS):
        pick = jnp.where(spread(rank[part * share : (part + 1) * share], slots), 1.0, 0.0)
        picks.append(pick.reshape(share * slots, rows_dev).astype(jnp.bfloat16))
    tiles_copy.wait()
    copies = []
    for part in range(PARTS):
        lines = pl.ds(part * share, share)
        rows = jnp.dot(picks[part], tiles_here[...], preferred_element_type=jnp.float32)
        out_here[lines] = rows.astype(jnp.bfloat16).reshape(share, slots, width)
        copies.append(pltpu.make_async_copy(out_here.at[lines], out_ref.at[lines], sems.at[2 + part]))
        copies[-1].start()
    for copy in copies:
        copy.wait()


def table_kernel(table_ref, out_ref):
    strips, rows_dev = table_ref.shape
    rows, positions = out_ref.shape
    slots = positions // strips
    low = rows_dev * lax.axis_index("strip")
    rank, place = places(table_ref[...], low, rows_dev)
    wide = jnp.broadcast_to(place[:, None, :], (strips, slots, rows_dev))
    named = jnp.where(spread(rank, slots), wide + 1, 0).astype(jnp.float32)
    named = named.reshape(positions, rows_dev).astype(jnp.bfloat16)
    ones = jnp.ones((16, rows_dev), jnp.bfloat16)
    target = lax.dot_general(ones, named, (((1,), (1,)), ((), ())), preferred_element_type=jnp.float32)
    target = jnp.broadcast_to(target[:1].astype(jnp.int32), (rows, positions))
    mine = lax.broadcasted_iota(jnp.int32, (rows, positions), 0) + 1
    out_ref[...] = jnp.where(target == mine, 1.0, 0.0).astype(jnp.bfloat16)


def unpack_kernel(offsets_ref, step_ref, table_ref, arrived_ref, ref_ref, slab_ref, strip):
    rows = ref_ref.shape[0]
    width = arrived_ref.shape[1]
    views = offsets_ref.shape[0]
    own = jnp.dot(table_ref[...], arrived_ref[...], preferred_element_type=jnp.float32)
    strip[:, :width] = own
    strip[:, width:] = jnp.zeros((rows, strip.shape[1] - width), jnp.float32)
    ref_ref[:, :128] = own[:, REF_FROM : REF_FROM + 128].astype(jnp.bfloat16)
    ref_ref[:, 128:] = strip[:, REF_FROM + 16 : REF_FROM + 144].astype(jnp.bfloat16)
    receiver = lax.rem(lax.axis_index("view") + views - lax.rem(step_ref[0], views), views)
    start = jnp.clip(OFF_MAX - offsets_ref[receiver, 0], 0, OFF_MAX)
    whole = start // 128
    part = start - whole * 128
    block = strip[:, pl.ds(pl.multiple_of(whole * 128, 128), 512)]
    turned = pltpu.roll(block, 512 - part, axis=1)
    near = lax.broadcasted_iota(jnp.int32, (16, 128), 0)
    unit = (near == lax.broadcasted_iota(jnp.int32, (16, 128), 1)).astype(jnp.bfloat16)
    rest = lax.dot_general(
        unit, turned[:, 256:384].astype(jnp.bfloat16), (((1,), (1,)), ((), ())), preferred_element_type=jnp.float32
    )
    rest = jnp.concatenate([rest[:8], jnp.zeros((8, 256 - rows), jnp.float32)], axis=1)
    slab_ref[...] = jnp.concatenate([turned[:, :256], rest], axis=0).astype(jnp.bfloat16)


def shards(images, offsets, pair_step, row_map):
    own_tiles = images[0]
    rows_dev, width = own_tiles.shape
    strips = lax.axis_size("strip")
    views = lax.axis_size("view")
    slots = slot_count(rows_dev, strips)
    rows = rows_dev + 2 * EDGE
    bf16 = jnp.bfloat16
    table = row_map.reshape(strips, rows_dev)
    anywhere = pl.BlockSpec(memory_space=pl.ANY)
    outgoing = pl.pallas_call(
        pack_kernel,
        out_shape=jax.ShapeDtypeStruct((strips, slots, width), bf16),
        in_specs=[anywhere, anywhere],
        out_specs=anywhere,
        scratch_shapes=[
            pltpu.VMEM((strips, rows_dev), jnp.int32),
            pltpu.VMEM((rows_dev, width), bf16),
            pltpu.VMEM((strips, slots, width), bf16),
            pltpu.SemaphoreType.DMA((2 + PARTS,)),
        ],
        name="pack",
    )(table, own_tiles)
    arrived = lax.all_to_all(outgoing, "strip", split_axis=0, concat_axis=0, tiled=True)
    select = pl.pallas_call(
        table_kernel, out_shape=jax.ShapeDtypeStruct((rows, strips * slots), bf16), name="table", compiler_params=SMALL
    )(table)
    smem = pl.BlockSpec(memory_space=pltpu.SMEM)
    vmem = pl.BlockSpec(memory_space=pltpu.VMEM)
    ref_rows, slab = pl.pallas_call(
        unpack_kernel,
        out_shape=(jax.ShapeDtypeStruct((rows, 256), bf16), jax.ShapeDtypeStruct((rows + 8, 256), bf16)),
        in_specs=[smem, smem, vmem, vmem],
        scratch_shapes=[pltpu.VMEM((rows, 768), jnp.float32)],
        compiler_params=SMALL,
        name="unpack",
    )(offsets, pair_step, select, arrived.reshape(strips * slots, width))

    def sent_by(step):
        return lambda rows_out: lax.ppermute(rows_out, "view", [(i, (i - step) % views) for i in range(views)])

    mate_rows = lax.switch(pair_step[0] % views - 1, [sent_by(step) for step in range(1, views)], slab)
    return cost(ref_rows, mate_rows)[None]


def solution(mesh):
    in_specs = (P("view", "strip", None), P(None, "strip"), P("strip"), P())
    out_specs = P("view", None, "strip", None)
    return jax.shard_map(shards, mesh=mesh, in_specs=in_specs, out_specs=out_specs, check_vma=False)
```

```python
import functools

import jax
import jax.numpy as jnp
from jax import lax
from jax.experimental import pallas as pl
from jax.experimental.pallas import tpu as pltpu
from jax.sharding import PartitionSpec as P

COLS = 128
DISP = 128
OFF_MAX = 376


EPSILON = 1e-05


RB = 16
PITCH = 17
PIECES = 2


def box_sums(values, weights):
    bf16 = jnp.bfloat16
    rows = values.shape[0]
    square = values * values
    high = square.astype(bf16).astype(jnp.float32)
    lines = jnp.concatenate([values, high, square - high], axis=0).astype(bf16)
    sums = jnp.dot(lines, weights, preferred_element_type=jnp.float32)
    return sums[:rows], sums[rows : 2 * rows] + sums[2 * rows :]


def cost_kernel(ref_ref, mate_ref, out_ref, ref32, mate32, base_a, base_b, lines_a, lines_b, last_a, last_b, sums_a, sums_b, sent, sems,
                mate_sum, mate_sq, ref_sum, ref_sq, stats, mate_here, mate_sem):
    step = pl.program_id(0)
    rows = ref_ref.shape[0]
    f32, bf16 = jnp.float32, jnp.bfloat16
    down = lax.broadcasted_iota(jnp.int32, (128, 128), 0)
    across = lax.broadcasted_iota(jnp.int32, (128, 128), 1)
    gap = across - down
    band_near = ((gap >= 0) & (gap <= 8)).astype(bf16)
    band_far = ((gap >= -16) & (gap <= -8) & (across >= 112)).astype(bf16)[112:]
    lane = lax.broadcasted_iota(jnp.int32, (8, 128), 1)
    lane_two = lax.broadcasted_iota(jnp.int32, (16, 128), 1)

    def skew(base, block, s):
        shift = 15 - s
        for t in range(2):
            part = block[t]
            if shift:
                part = pltpu.roll(jnp.where(lane_two < shift, block[t + 1], part), 128 - shift, axis=1)
            part = part.astype(f32)
            for r in range(0, RB, 8):
                base[t, pl.ds(r * PITCH + s, 8, stride=PITCH), :] = part[r : r + 8]

    def lines_from(first):
        block = mate32[pl.ds(first, RB), :].astype(bf16)
        return [block[:, 128 * t : 128 * t + 128] for t in range(3)]

    def one_line(base, first, r):
        tiles = [base[t, pl.ds(r * PITCH, 16), :].astype(bf16) for t in range(2)]
        parts = []
        for p in range(-1, 8):
            shift = 112 - 16 * p
            if shift in (0, 128):
                part = tiles[shift // 128]
            else:
                part = pltpu.roll(jnp.where(lane_two < shift, tiles[1], tiles[0]), 128 - shift, axis=1)
            parts.append(part)
        near = jnp.concatenate(parts[1:], axis=0)
        far = jnp.concatenate(parts[:-1], axis=0)
        row = ref32[pl.ds(first + r, 1), :].astype(bf16)
        left = jnp.concatenate([near, far], axis=1)
        beyond = jnp.concatenate(
            [jnp.zeros((112, 128), bf16), band_far * jnp.broadcast_to(row[:, 128:], (16, 128))], axis=0
        )
        right = jnp.concatenate([band_near * jnp.broadcast_to(row[:, :128], (128, 128)), beyond], axis=1)
        return lax.dot_general(left, right, (((1,), (1,)), ((), ())), preferred_element_type=f32)

    @pl.when(step == 0)
    def _():
        arrival = pltpu.make_async_copy(mate_ref, mate_here, mate_sem)
        arrival.start()

        def window(ref):
            x = [ref[i : i + rows - 8, :] for i in range(9)]
            return ((x[0] + x[1]) + (x[2] + x[3])) + ((x[4] + x[5]) + (x[6] + x[7])) + x[8]

        def inverse(total, total_sq):
            mean = total / 81.0
            return lax.rsqrt(jnp.maximum(total_sq / 81.0 - mean * mean, 0.0) + EPSILON)

        ref32[:rows] = ref_ref[...].astype(f32)
        ref32[rows:] = jnp.zeros((16, 256), f32)
        mate32[rows:] = jnp.zeros((32, 384), f32)
        k = lax.broadcasted_iota(jnp.int32, (256, 128), 0)
        gap_ref = jnp.where(k < 128, k, k - 112) - lax.broadcasted_iota(jnp.int32, (256, 128), 1)
        weights = ((gap_ref >= 0) & (gap_ref <= 8) & ((k < 128) | (k >= 240))).astype(bf16)
        ref_sum[...], ref_sq[...] = box_sums(ref32[:rows], weights)
        total = window(ref_sum)
        stats[4] = total / 81.0
        stats[5] = inverse(total, window(ref_sq))
        k = lax.broadcasted_iota(jnp.int32, (256, 256), 0)
        c = lax.broadcasted_iota(jnp.int32, (256, 256), 1)
        weights = ((k - c >= 0) & (k - c <= 8)).astype(bf16)
        k, c = k[:16] + 256, c[:16]
        beyond = jnp.where((k - c >= 0) & (k - c <= 8), 1.0, 0.0)
        beyond = jnp.concatenate([beyond, jnp.zeros((112, 256), f32)], axis=0).astype(bf16)
        weights = jnp.concatenate([weights, beyond], axis=0)
        same = lax.broadcasted_iota(jnp.int32, (rows, 256), 0) == lax.broadcasted_iota(jnp.int32, (rows, 256), 1)
        same = same.astype(bf16)
        arrival.wait()
        held = mate_here[...].astype(f32)
        rest = jnp.concatenate([held[rows:], jnp.zeros((120, 256), f32)], axis=0).astype(bf16)
        mate32[:rows, :256] = held[:rows]
        mate32[:rows, 256:] = lax.dot_general(same, rest, (((1,), (1,)), ((), ())), preferred_element_type=f32)
        total, total_sq = box_sums(mate32[:rows], weights)
        for t in range(2):
            mate_sum[t] = total[:, 128 * t : 128 * t + 128]
            mate_sq[t] = total_sq[:, 128 * t : 128 * t + 128]
        for base, first in ((base_b, 0), (base_a, 8)):
            block = lines_from(first)
            for s in range(16):
                skew(base, block, s)
        for r in range(8):
            last_a[r] = one_line(base_b, 0, r)
        for r in range(16):
            lines_a[r] = one_line(base_a, 8, r)
        block = lines_from(24)
        for s in range(16):
            skew(base_b, block, s)

        for t in range(2):
            total = window(mate_sum.at[t])
            stats[t] = total
            stats[2 + t] = inverse(total, window(mate_sq.at[t])) / 81.0

    def copy(block, half, piece):
        size = DISP // PIECES
        return pltpu.make_async_copy(
            sent.at[half, pl.ds(piece * size, size)],
            out_ref.at[pl.ds(piece * size, size), pl.ds(pl.multiple_of(block * RB, RB), RB), :],
            sems.at[half, piece],
        )

    def half_step(half, last_in, lines, last_out, lines_next, base, base_next):
        block = 2 * step + half
        first = pl.multiple_of(block * RB, RB)
        ahead = first + RB + 8

        @pl.when(step > 0)
        def _():
            for piece in range(PIECES):
                copy(block, half, piece).wait()

        block_next = lines_from(pl.multiple_of(ahead + RB, 8))

        def vertical(q, sums):
            h = [last_in[i, 8 * q : 8 * q + 8, :] for i in range(8)]
            h += [lines[i, 8 * q : 8 * q + 8, :] for i in range(RB)]
            for i in range(8):
                last_out[i, 8 * q : 8 * q + 8, :] = h[RB + i]
            for begin in range(0, RB, 9):
                suffix = [None] * 8 + [h[begin + 8]]
                for i in range(7, -1, -1):
                    suffix[i] = h[begin + i] + suffix[i + 1]
                prefix = None
                for i in range(min(9, RB - begin)):
                    total = suffix[i]
                    if i:
                        nxt = h[begin + 8 + i]
                        prefix = nxt if prefix is None else prefix + nxt
                        total = total + prefix
                    sums[pl.ds(begin + i, 8, stride=PITCH), :] = total

        def normalize(q, sums):
            for j in range(8):
                k = 8 * q + j
                done = []
                for u in range(0, RB, 8):
                    m0, m1, v0, v1, ref_mean, ref_inv = [
                        stats[i, pl.ds(pl.multiple_of(first + u, 8), 8), :] for i in range(6)
                    ]
                    mean, scale = m0, v0
                    if k < 127:
                        mean = pltpu.roll(jnp.where(lane >= 127 - k, m0, m1), k + 1, axis=1)
                        scale = pltpu.roll(jnp.where(lane >= 127 - k, v0, v1), k + 1, axis=1)
                    total = sums[pl.ds(j * PITCH + u, 8), :]
                    done.append((total - ref_mean * mean) * ref_inv * scale)
                sent[half, k] = jnp.concatenate(done, axis=0).astype(bf16)
            if (q + 1) % (16 // PIECES) == 0:
                copy(block, half, q // (16 // PIECES)).start()

        both = (sums_a, sums_b)
        for q in range(16):
            lines_next[q] = one_line(base, ahead, q)
            skew(base_next, block_next, q)
            vertical(q, both[q % 2])
            if q:
                normalize(q - 1, both[(q - 1) % 2])
        normalize(15, both[1])

    half_step(0, last_a, lines_a, last_b, lines_b, base_b, base_a)
    half_step(1, last_b, lines_b, last_a, lines_a, base_a, base_b)

    @pl.when(step == pl.num_programs(0) - 1)
    def _():
        for half in range(2):
            for piece in range(PIECES):
                copy(0, half, piece).wait()


def cost(ref_rows, mate_rows):
    rows = ref_rows.shape[0]
    f32 = jnp.float32
    vmem = pl.BlockSpec(memory_space=pltpu.VMEM)
    return pl.pallas_call(
        cost_kernel,
        out_shape=jax.ShapeDtypeStruct((DISP, rows - 8, COLS), jnp.bfloat16),
        grid=((rows - 8) // (2 * RB),),
        in_specs=[vmem, pl.BlockSpec(memory_space=pl.ANY)],
        out_specs=pl.BlockSpec(memory_space=pl.ANY),
        scratch_shapes=[
            pltpu.VMEM((rows + 16, 256), f32),
            pltpu.VMEM((rows + 32, 384), f32),
            pltpu.VMEM((2, 16 * PITCH + 24, 128), f32),
            pltpu.VMEM((2, 16 * PITCH + 24, 128), f32),
            pltpu.VMEM((RB, 128, 128), f32),
            pltpu.VMEM((RB, 128, 128), f32),
            pltpu.VMEM((8, 128, 128), f32),
            pltpu.VMEM((8, 128, 128), f32),
            pltpu.VMEM((8 * PITCH + 24, 128), f32),
            pltpu.VMEM((8 * PITCH + 24, 128), f32),
            pltpu.VMEM((2, DISP, RB, COLS), jnp.bfloat16),
            pltpu.SemaphoreType.DMA((2, PIECES)),
            pltpu.VMEM((2, rows, 128), f32),
            pltpu.VMEM((2, rows, 128), f32),
            pltpu.VMEM((rows, 128), f32),
            pltpu.VMEM((rows, 128), f32),
            pltpu.VMEM((6, rows - 8, 128), f32),
            pltpu.VMEM(mate_rows.shape, mate_rows.dtype),
            pltpu.SemaphoreType.DMA,
        ],
        compiler_params=pltpu.CompilerParams(dimension_semantics=("arbitrary",), vmem_limit_bytes=16 << 20),
        name="cost_volume",
    )(ref_rows, mate_rows)


SPAN = COLS + DISP + 8
EDGE = 4
PARTS = 4
SMALL = pltpu.CompilerParams(vmem_limit_bytes=16 << 20)
REF_FROM = OFF_MAX + DISP - 1


def slot_count(rows_dev, strips):
    wide = rows_dev // strips + 2 * EDGE
    return -(-wide // 8) * 8


def places(ids, low, rows_dev):
    line = ids.shape[1]
    place = ids - low + EDGE
    wanted = (place >= 0) & (place < rows_dev + 2 * EDGE)
    before = lax.broadcasted_iota(jnp.int32, (line, line), 0)
    after = lax.broadcasted_iota(jnp.int32, (line, line), 1)
    earlier = (before < after).astype(jnp.bfloat16)
    flags = jnp.where(wanted, 1.0, 0.0)
    pad = (-flags.shape[0]) % 16
    if pad:
        flags = jnp.concatenate([flags, jnp.zeros((pad, line), jnp.float32)], axis=0)
    rank = jnp.dot(flags.astype(jnp.bfloat16), earlier, preferred_element_type=jnp.float32)
    rank = rank[: ids.shape[0]].astype(jnp.int32)
    return jnp.where(wanted, rank, -1), place


def spread(rank, slots):
    strips, line = rank.shape
    wide = jnp.broadcast_to(rank[:, None, :], (strips, slots, line))
    return wide == lax.broadcasted_iota(jnp.int32, (strips, slots, line), 1)


def pack_kernel(near_cores, map_ref, tiles_ref, *refs):
    out_refs, (map_here, tiles_here, out_here, sems) = refs[:-4], refs[-4:]
    strips, slots, width = out_here.shape
    rows_dev = tiles_ref.shape[0]
    map_copy = pltpu.make_async_copy(map_ref, map_here, sems.at[0])
    tiles_copy = pltpu.make_async_copy(tiles_ref, tiles_here, sems.at[1])
    map_copy.start()
    tiles_copy.start()
    map_copy.wait()
    ids = jnp.broadcast_to(map_here[pl.ds(lax.axis_index("strip"), 1), :], (strips, rows_dev))
    line = lax.broadcasted_iota(jnp.int32, (strips, rows_dev), 0)
    target = jnp.bitwise_xor(line, lax.axis_index("strip")) if near_cores else line
    rank, _ = places(ids, rows_dev * target, rows_dev)
    share = strips // PARTS
    picks = []
    for part in range(PARTS):
        pick = jnp.where(spread(rank[part * share : (part + 1) * share], slots), 1.0, 0.0)
        picks.append(pick.reshape(share * slots, rows_dev).astype(jnp.bfloat16))
    tiles_copy.wait()
    copies = []
    for part in reversed(range(PARTS)):
        lines = pl.ds(part * share, share)
        rows = jnp.dot(picks[part], tiles_here[...], preferred_element_type=jnp.float32)
        out_here[lines] = rows.astype(jnp.bfloat16).reshape(share, slots, width)
        if near_cores and part:
            moves = [(out_here.at[lines], out_refs[part + 1])]
        elif near_cores:
            moves = [(out_here.at[0], out_refs[0]), (out_here.at[1], out_refs[1])]
        else:
            moves = [(out_here.at[lines], out_refs[0].at[lines])]
        for source, place in moves:
            copies.append(pltpu.make_async_copy(source, place, sems.at[2 + len(copies)]))
            copies[-1].start()
    for copy in copies:
        copy.wait()


def table_kernel(near_cores, table_ref, own_ref, out_ref, own_here, sem):
    own_copy = pltpu.make_async_copy(own_ref, own_here, sem)
    own_copy.start()
    strips, rows_dev = table_ref.shape
    rows, positions = out_ref.shape
    slots = positions // strips
    me = lax.axis_index("strip")
    ids = table_ref[...]
    if near_cores:
        order = list(range(0, strips, 2)) + list(range(1, strips, 2))
        ids = jnp.concatenate([table_ref[pl.ds(jnp.bitwise_xor(me, line), 1), :] for line in order], axis=0)
    rank, place = places(ids, rows_dev * me, rows_dev)
    wide = jnp.broadcast_to(place[:, None, :], (strips, slots, rows_dev))
    named = jnp.where(spread(rank, slots), wide + 1, 0).astype(jnp.float32)
    named = named.reshape(positions, rows_dev).astype(jnp.bfloat16)
    ones = jnp.ones((16, rows_dev), jnp.bfloat16)
    target = lax.dot_general(ones, named, (((1,), (1,)), ((), ())), preferred_element_type=jnp.float32)
    target = jnp.broadcast_to(target[:1].astype(jnp.int32), (rows, positions))
    mine = lax.broadcasted_iota(jnp.int32, (rows, positions), 0) + 1
    out_ref[...] = jnp.where(target == mine, 1.0, 0.0).astype(jnp.bfloat16)
    own_copy.wait()


def unpack_kernel(starts_ref, step_ref, table_ref, *refs):
    arrived_refs, (ref_ref, slab_ref, strip) = refs[:-3], refs[-3:]
    rows = ref_ref.shape[0]
    width = arrived_refs[0].shape[1]
    views = starts_ref.shape[0]
    arrived = arrived_refs[0][...]
    if len(arrived_refs) > 1:
        arrived = jnp.concatenate([ref[...].astype(jnp.float32) for ref in arrived_refs], axis=0).astype(jnp.bfloat16)
    own = jnp.dot(table_ref[...], arrived, preferred_element_type=jnp.float32)
    strip[:, :width] = own
    strip[:, width:] = jnp.zeros((rows, strip.shape[1] - width), jnp.float32)
    ref_ref[:, :128] = own[:, REF_FROM : REF_FROM + 128].astype(jnp.bfloat16)
    ref_ref[:, 128:] = strip[:, REF_FROM + 16 : REF_FROM + 144].astype(jnp.bfloat16)
    receiver = lax.rem(lax.axis_index("view") + views - lax.rem(step_ref[0], views), views)
    start = jnp.clip(starts_ref[receiver], 0, OFF_MAX)
    whole = start // 128
    part = start - whole * 128
    block = strip[:, pl.ds(pl.multiple_of(whole * 128, 128), 512)]
    turned = pltpu.roll(block, 512 - part, axis=1)
    near = lax.broadcasted_iota(jnp.int32, (16, 128), 0)
    unit = (near == lax.broadcasted_iota(jnp.int32, (16, 128), 1)).astype(jnp.bfloat16)
    rest = lax.dot_general(
        unit, turned[:, 256:384].astype(jnp.bfloat16), (((1,), (1,)), ((), ())), preferred_element_type=jnp.float32
    )
    rest = jnp.concatenate([rest[:8], jnp.zeros((8, 256 - rows), jnp.float32)], axis=1)
    slab_ref[...] = jnp.concatenate([turned[:, :256], rest], axis=0).astype(jnp.bfloat16)


def shards(images, offsets, pair_step, row_map):
    own_tiles = images[0]
    rows_dev, width = own_tiles.shape
    strips = lax.axis_size("strip")
    views = lax.axis_size("view")
    slots = slot_count(rows_dev, strips)
    rows = rows_dev + 2 * EDGE
    bf16 = jnp.bfloat16
    near_cores = strips == 8
    table = row_map.reshape(strips, rows_dev)
    shapes = [(strips, slots, width)]
    if near_cores:
        shapes = [(slots, width)] * 2 + [(2, slots, width)] * 3
    anywhere = pl.BlockSpec(memory_space=pl.ANY)
    outgoing = pl.pallas_call(
        functools.partial(pack_kernel, near_cores),
        out_shape=[jax.ShapeDtypeStruct(shape, bf16) for shape in shapes],
        in_specs=[anywhere, anywhere],
        out_specs=[anywhere] * len(shapes),
        scratch_shapes=[
            pltpu.VMEM((strips, rows_dev), jnp.int32),
            pltpu.VMEM((rows_dev, width), bf16),
            pltpu.VMEM((strips, slots, width), bf16),
            pltpu.SemaphoreType.DMA((3 + PARTS,)),
        ],
        name="pack",
    )(table, own_tiles)
    vmem = pl.BlockSpec(memory_space=pltpu.VMEM)
    own_shape = (slots, width)
    select, own = pl.pallas_call(
        functools.partial(table_kernel, near_cores),
        out_shape=[jax.ShapeDtypeStruct((rows, strips * slots), bf16), jax.ShapeDtypeStruct(own_shape, bf16)],
        in_specs=[vmem, anywhere],
        out_specs=[vmem, vmem],
        scratch_shapes=[pltpu.SemaphoreType.DMA],
        name="table",
        compiler_params=SMALL,
    )(table, outgoing[0] if near_cores else outgoing[0][0])
    starts = OFF_MAX - offsets[:, 0]
    if near_cores:

        def swapped(value, by):
            return lax.ppermute(value, "strip", [(i, i ^ by) for i in range(strips)])

        got = [swapped(outgoing[d + 1], 2 * d) for d in range(1, 4)]
        select, own, starts, got[0] = lax.optimization_barrier((select, own, starts, got[0]))
        arrived = [own] + [pair[0] for pair in got]
        arrived += [swapped(outgoing[1], 1)] + [swapped(pair[1], 1) for pair in got]
    else:
        arrived = [lax.all_to_all(outgoing[0], "strip", split_axis=0, concat_axis=0, tiled=True).reshape(-1, width)]
    smem = pl.BlockSpec(memory_space=pltpu.SMEM)
    ref_rows, slab = pl.pallas_call(
        unpack_kernel,
        out_shape=(jax.ShapeDtypeStruct((rows, 256), bf16), jax.ShapeDtypeStruct((rows + 8, 256), bf16)),
        in_specs=[smem, smem, vmem] + [vmem] * len(arrived),
        scratch_shapes=[pltpu.VMEM((rows, 768), jnp.float32)],
        compiler_params=SMALL,
        name="unpack",
    )(starts, pair_step, select, *arrived)

    def sent_by(step):
        return lambda rows_out: lax.ppermute(rows_out, "view", [(i, (i - step) % views) for i in range(views)])

    mate_rows = lax.switch(pair_step[0] % views - 1, [sent_by(step) for step in range(1, views)], slab)
    return cost(ref_rows, mate_rows)[None]


def solution(mesh):
    in_specs = (P("view", "strip", None), P(None, "strip"), P("strip"), P())
    out_specs = P("view", None, "strip", None)
    return jax.shard_map(shards, mesh=mesh, in_specs=in_specs, out_specs=out_specs, check_vma=False)
```
